32 devices in a mesh: fsdp: 16 (over z, y, x), tp: 2 (over core).
Axes of the slice: x: 2, y: 2, z: 4, core: 2. Of those that a mesh axis runs over, the one named last changes fastest.
Arguments:
- tokens: bfloat16 [2, 2048, 8192], P(None, 'fsdp', 'tp'), may hold values from -6 to 6
- frozen_weight: bfloat16 [8192, 2048], P('tp', 'fsdp'), may hold values from -0.0625 to 0.0625
- cotangent: bfloat16 [2, 2048, 2048], P(None, 'fsdp'), may hold values from -6 to 6
- block_adapter_index: int32 [2, 16], replicated, may hold values from 0 to 511
- down_weight: bfloat16 [512, 8192, 16], P(None, ('tp', 'fsdp')), may hold values from -0.0625 to 0.0625
- up_weight: bfloat16 [512, 16, 2048], P(None, None, ('tp', 'fsdp')), may hold values from -0.125 to 0.125
Outputs:
- key_value_output: bfloat16 [2, 2048, 2048], P(None, 'fsdp', 'tp')
- input_gradient: bfloat16 [2, 2048, 8192], P(None, 'fsdp', 'tp')
- grad_down: float32 [512, 8192, 16], P(None, ('tp', 'fsdp'))
- up_weight_gradient: float32 [512, 16, 2048], P(None, None, ('tp', 'fsdp'))
The draws below stay inside these ranges and needn't reach their ends.
Inputs may be any that keep to these rules, and one draw needn't show every extreme that they name: `block_adapter_index`: one adapter for each block of 128 rows of a microbatch.
All inputs are finite; a program needn't handle non-finite values.
Results may differ from the reference program's by a relative error of at most 0.005.
Values may be sent and summed in bfloat16 or wider, within the bound.
No kernel may reach another device: no remote copies, remote signals or barrier semaphores. Data moves between devices by JAX's collectives and lax.ppermute only.
A program may use at most 128 MiB of HBM per device.

```python
import math
import jax
import jax.numpy as jnp
import numpy as np

MODEL_WIDTH = 8192
ADAPTER_RANK = 16
ADAPTER_TOTAL = 512
BLOCK = 128
MICROBATCH_COUNT = 2
KEY_VALUE_WIDTH = 2048
TOKEN_ROWS = 2048
BLOCKS_PER_BATCH = 16


def set_ends(result, rng, smallest, top_value):
    longest = result.shape.index(max(result.shape))
    spots = []
    for shift in (0, 1):
        where = [jax.random.randint(jax.random.fold_in(rng, axis), (), 0, length) for axis, length in enumerate(result.shape)]
        where[longest] = (where[longest] + shift) % result.shape[longest]
        spots.append(tuple(where))
    return result.at[spots[0]].set(smallest).at[spots[1]].set(top_value)


def level_of(own_key, dims, pieces, smallest, largest):
    def one(axis_at, parts):
        draws = jax.random.uniform(jax.random.fold_in(jax.random.fold_in(own_key, 6), axis_at), (parts,), jnp.float32, smallest / len(pieces), largest / len(pieces))
        return jnp.repeat(jnp.exp(draws), dims[axis_at] // parts).reshape((-1,) + (1,) * (len(dims) - axis_at - 1))

    factor_of = one(*pieces[0])
    for cut in pieces[1:]:
        factor_of = factor_of * one(*cut)
    return factor_of


def rank_bounds(amount, skew):
    weights = [(1 << 20) // math.isqrt(grade ** skew) + 1 for grade in range(1, amount + 1)]
    width = 1 + sum(weights) // (1 << 30)
    return np.cumsum(np.array([max(1, weight // width) for weight in weights]))


def skewed_ids(rng, shape, amount, lean):
    grid = rank_bounds(amount, lean)
    ticket = jax.random.randint(jax.random.fold_in(rng, 1), shape, 0, int(grid[amount - 1]))
    grade = jnp.searchsorted(jnp.asarray(grid, jnp.int32), ticket, side="right")
    return jax.random.permutation(jax.random.fold_in(rng, 2), amount)[grade].astype(jnp.int32)


def centred(rng, extent, deviation, reach, pieces=(), kind=jnp.bfloat16):
    values = jax.random.normal(rng, extent, jnp.float32) * deviation
    if len(pieces) > 0:
        values = level_of(rng, extent, pieces, -0.22, 0.18) * values
    return jnp.clip(values, min=-reach, max=reach).astype(kind)


def setup_inputs(seed: int = 0) -> dict:
    keys = jax.random.split(jax.random.key(seed), 7)
    return {
        "tokens": centred(keys[0], (MICROBATCH_COUNT, TOKEN_ROWS, MODEL_WIDTH), 1.0, 6.0, ((1, 16), (2, 2))),
        "frozen_weight": centred(keys[1], (MODEL_WIDTH, KEY_VALUE_WIDTH), MODEL_WIDTH ** -0.5, 0.0625, ((0, 2), (1, 16))),
        "cotangent": centred(keys[2], (MICROBATCH_COUNT, TOKEN_ROWS, KEY_VALUE_WIDTH), 1.0, 6.0, ((1, 16),)),
        "block_adapter_index": set_ends(skewed_ids(keys[3], (MICROBATCH_COUNT, BLOCKS_PER_BATCH), ADAPTER_TOTAL, 2), jax.random.fold_in(keys[3], 3), 0, ADAPTER_TOTAL - 1).astype(jnp.int32),
        "down_weight": centred(keys[4], (ADAPTER_TOTAL, MODEL_WIDTH, ADAPTER_RANK), MODEL_WIDTH ** -0.5, 0.0625, ((1, 32),)),
        "up_weight": centred(keys[5], (ADAPTER_TOTAL, ADAPTER_RANK, KEY_VALUE_WIDTH), KEY_VALUE_WIDTH ** -0.5, 0.125, ((2, 32),)),
    }


adapter_scale = 2.0


def reference(tokens, frozen_weight, cotangent, block_adapter_index, down_weight, up_weight):
    tok_matrix = tokens.reshape(MICROBATCH_COUNT * TOKEN_ROWS, MODEL_WIDTH)
    cot_matrix = cotangent.reshape(MICROBATCH_COUNT * TOKEN_ROWS, KEY_VALUE_WIDTH)
    frozen_key_value = jnp.dot(tok_matrix, frozen_weight, preferred_element_type=jnp.float32)
    frozen_input_gradient = jnp.dot(cot_matrix, frozen_weight.T, preferred_element_type=jnp.float32)
    tok_blocks = tokens.reshape(MICROBATCH_COUNT, BLOCKS_PER_BATCH, BLOCK, MODEL_WIDTH).astype(jnp.float32)
    gradient_blocks = cotangent.reshape(MICROBATCH_COUNT, BLOCKS_PER_BATCH, BLOCK, KEY_VALUE_WIDTH).astype(jnp.float32)
    down_weight_rows = jnp.take(down_weight, block_adapter_index, axis=0).astype(jnp.float32)
    up_weight_rows = jnp.take(up_weight, block_adapter_index, axis=0).astype(jnp.float32)
    low_rank = jnp.einsum("mnbd,mndr->mnbr", tok_blocks, down_weight_rows).astype(jnp.bfloat16)
    rank_gradient = (adapter_scale * jnp.einsum("fsvj,fsyj->fsvy", gradient_blocks, up_weight_rows)).astype(jnp.bfloat16)
    rank_wide_product = low_rank.astype(jnp.float32)
    wide_input_gradient = rank_gradient.astype(jnp.float32)
    adapter_key_value = (adapter_scale * jnp.einsum("elui,elis->elus", rank_wide_product, up_weight_rows)).astype(jnp.bfloat16)
    adapter_input_gradient = jnp.einsum("gwef,gwhf->gweh", wide_input_gradient, down_weight_rows).astype(jnp.bfloat16)
    key_value_output = (frozen_key_value.reshape(MICROBATCH_COUNT, TOKEN_ROWS, KEY_VALUE_WIDTH) + adapter_key_value.reshape(MICROBATCH_COUNT, TOKEN_ROWS, KEY_VALUE_WIDTH).astype(jnp.float32)).astype(jnp.bfloat16)
    input_gradient = (frozen_input_gradient.reshape(MICROBATCH_COUNT, TOKEN_ROWS, MODEL_WIDTH) + adapter_input_gradient.reshape(MICROBATCH_COUNT, TOKEN_ROWS, MODEL_WIDTH).astype(jnp.float32)).astype(jnp.bfloat16)
    down_tiles = jnp.einsum("mnbd,mnbr->mndr", tok_blocks, wide_input_gradient).reshape(MICROBATCH_COUNT * BLOCKS_PER_BATCH, MODEL_WIDTH, ADAPTER_RANK)
    up_weight_tiles = (adapter_scale * jnp.einsum("puai,puac->puic", rank_wide_product, gradient_blocks)).reshape(MICROBATCH_COUNT * BLOCKS_PER_BATCH, ADAPTER_RANK, KEY_VALUE_WIDTH)
    block_indices = block_adapter_index.reshape(-1).astype(jnp.int32)
    grad_down = jax.ops.segment_sum(down_tiles, block_indices, num_segments=ADAPTER_TOTAL)
    up_weight_gradient = jax.ops.segment_sum(up_weight_tiles, block_indices, num_segments=ADAPTER_TOTAL)
    return key_value_output, input_gradient, grad_down, up_weight_gradient
```

```python
import functools

import jax
import jax.numpy as jnp
from jax import lax
from jax.experimental import pallas as pl
from jax.experimental.pallas import tpu as pltpu
from jax.sharding import PartitionSpec as P

BLOCK = 128
LANES = 128

adapter_scale = 2.0


def selected_sum(adapter_selector, tiles):
    flat = tiles.reshape(tiles.shape[0], -1)
    return lax.dot_general(
        adapter_selector,
        flat,
        (((0,), (0,)), ((), ())),
        precision=lax.Precision.HIGHEST,
        preferred_element_type=jnp.float32,
    )


def pick(flag, first, second):
    return jnp.where(flag, first, second)


def send(value, axis, count, route):
    return lax.ppermute(value, axis, [(i, route(i)) for i in range(count)])


def chunk_kernel(first, block_count, width, start, columns_ref, *refs):
    blocks = refs[:block_count]
    tok_own, tok_pair, cot_own, cot_pair, kv_in = refs[block_count : block_count + 5]
    ig_own, ig_pair, kv_out = refs[block_count + 5 : block_count + 8]
    weight, tok, cot, sems = refs[block_count + 8 :]
    rows = tok_own.shape[0]
    depth = weight.shape[0]
    copies = [
        pltpu.make_async_copy(
            tok_own.at[:, pl.ds(start, depth)], tok.at[pl.ds(0, rows), :], sems.at[block_count]
        ),
        pltpu.make_async_copy(
            tok_pair.at[:, pl.ds(start, depth)], tok.at[pl.ds(rows, rows), :], sems.at[block_count + 1]
        ),
        pltpu.make_async_copy(cot_own, cot.at[pl.ds(0, rows), :], sems.at[block_count + 2]),
        pltpu.make_async_copy(cot_pair, cot.at[pl.ds(rows, rows), :], sems.at[block_count + 3]),
    ]
    block_copies = []
    for i, block in enumerate(blocks):
        column = pl.multiple_of(columns_ref[i] * width, width)
        block_copies.append(
            pltpu.make_async_copy(block, weight.at[:, pl.ds(column, width)], sems.at[i])
        )
    for copy in copies[:2] + block_copies + copies[2:]:
        copy.start()
    copies[0].wait()
    copies[1].wait()
    for i, copy in enumerate(block_copies):
        copy.wait()
        column = pl.multiple_of(columns_ref[i] * width, width)
        part = jnp.dot(
            tok[...], weight[:, pl.ds(column, width)], preferred_element_type=jnp.float32
        )
        if not first:
            part = part + kv_in[:, pl.ds(column, width)]
        kv_out[:, pl.ds(column, width)] = part
    copies[2].wait()
    copies[3].wait()
    tile = min(2 * LANES, depth)

    @pl.loop(0, depth // tile)
    def _(step):
        at = pl.multiple_of(step * tile, tile)
        part = lax.dot_general(
            cot[...],
            weight[pl.ds(at, tile), :],
            (((1,), (1,)), ((), ())),
            preferred_element_type=jnp.float32,
        )
        ig_own[:, pl.ds(at, tile)] = part[:rows]
        ig_pair[:, pl.ds(at, tile)] = part[rows:].astype(ig_pair.dtype)


def chunk_product(columns, blocks, tok_own, tok_pair, cot_own, cot_pair, kv, start, name):
    rows = tok_own.shape[0]
    depth, width = blocks[0].shape
    total = cot_own.shape[1]
    count = len(blocks)
    first = kv is None
    kv_shape = jax.ShapeDtypeStruct((2 * rows, total), jnp.float32)
    if first:
        kv = jnp.zeros((8, LANES), jnp.float32)
    anywhere = pl.BlockSpec(memory_space=pl.ANY)
    vmem = pl.BlockSpec(memory_space=pltpu.VMEM)
    flops = 8 * rows * depth * total
    return pl.pallas_call(
        functools.partial(chunk_kernel, first, count, width, start),
        name=name,
        out_shape=(
            jax.ShapeDtypeStruct((rows, depth), jnp.float32),
            jax.ShapeDtypeStruct((rows, depth), jnp.bfloat16),
            kv_shape,
        ),
        in_specs=[pl.BlockSpec(memory_space=pltpu.SMEM)] + [anywhere] * (count + 4) + [vmem],
        out_specs=(vmem, vmem, vmem),
        scratch_shapes=[
            pltpu.VMEM((depth, total), jnp.bfloat16),
            pltpu.VMEM((2 * rows, depth), jnp.bfloat16),
            pltpu.VMEM((2 * rows, total), jnp.bfloat16),
            pltpu.SemaphoreType.DMA((count + 4,)),
        ],
        cost_estimate=pl.CostEstimate(
            flops=flops,
            bytes_accessed=2 * depth * total + 6 * rows * total + 16 * rows * total,
            transcendentals=0,
        ),
        compiler_params=pltpu.CompilerParams(vmem_limit_bytes=56 * 1024 * 1024),
    )(columns, *blocks, tok_own, tok_pair, cot_own, cot_pair, kv)


def paired_base(tok, frozen_weight, cot):
    count = lax.axis_size("fsdp")
    layers = count // 4
    index = lax.axis_index("fsdp")
    core = lax.axis_index("tp")
    x, y, z = index % 2, (index // 2) % 2, index // 4
    rows, shard = tok.shape
    half = shard // 2
    total = cot.shape[1]
    low = x == 0
    left = core == 0

    x_send = lambda v: send(v, "fsdp", count, lambda i: i ^ 1)
    y_send = lambda v: send(v, "fsdp", count, lambda i: i ^ 2)
    z_send = lambda v: send(v, "fsdp", count, lambda i: (i + 4) % count)
    core_send = lambda v: send(v, "tp", 2, lambda i: i ^ 1)

    chunks = ((0, 3 * half // 4, "zy"), (3 * half // 4, half // 4, "yz"))
    pair_blocks = []
    for start, depth, _ in chunks:
        mine = pick(low, frozen_weight[start : start + depth], frozen_weight[half + start : half + start + depth])
        other = pick(low, frozen_weight[half + start : half + start + depth], frozen_weight[start : start + depth])
        got = x_send(other)
        pair_blocks.append(
            jnp.concatenate([pick(low, mine, got), pick(low, got, mine)], axis=1)
        )
    tok_own = pick(low, tok[:, :half], tok[:, half:])
    tok_pair = x_send(pick(low, tok[:, half:], tok[:, :half]))
    cot_part = x_send(pick(left, cot[:, : total // 2], cot[:, total // 2 :]))
    cot_rest = core_send(cot_part)
    cot_pair = jnp.concatenate(
        [pick(left, cot_part, cot_rest), pick(left, cot_rest, cot_part)], axis=1
    )

    kv = None
    own_pieces, sent_pieces = [], []
    for (start, depth, order), block in zip(chunks, pair_blocks):
        blocks, columns = [], []
        if order == "zy":
            held = block
            for step in range(layers):
                if step:
                    held = z_send(held)
                place = (z - step) % layers
                blocks += [held, y_send(held)]
                columns += [place * 2 + y, place * 2 + 1 - y]
        else:
            held = jnp.concatenate([block, y_send(block)], axis=0)
            for step in range(layers):
                if step:
                    held = z_send(held)
                place = (z - step) % layers
                blocks += [held[:depth], held[depth:]]
                columns += [place * 2 + y, place * 2 + 1 - y]
        own, pair, kv = chunk_product(
            jnp.stack(columns).astype(jnp.int32),
            blocks,
            tok_own,
            tok_pair,
            cot,
            cot_pair,
            kv,
            start,
            f"base_{start}",
        )
        own_pieces.append(own)
        sent_pieces.append(x_send(pair))
    own_half = jnp.concatenate(own_pieces, axis=1)
    got_half = jnp.concatenate(sent_pieces, axis=1).astype(jnp.float32)
    gradient_base = jnp.concatenate(
        [pick(low, own_half, got_half), pick(low, got_half, own_half)], axis=1
    )
    lower, upper = kv[:, : total // 2], kv[:, total // 2 :]
    core_got = core_send(pick(left, upper, lower).astype(jnp.bfloat16))
    kv_here = pick(left, lower, upper) + core_got.astype(jnp.float32)
    kv_got = x_send(kv_here[rows:].astype(jnp.bfloat16))
    kv_base = kv_here[:rows] + kv_got.astype(jnp.float32)
    return kv_base, gradient_base


def plain_base(tok, frozen_weight, cot):
    gathered = lax.all_gather(frozen_weight, "fsdp", axis=1, tiled=True)
    kv_partial = jnp.dot(tok, gathered, preferred_element_type=jnp.float32)
    kv_base = lax.psum_scatter(kv_partial, "tp", scatter_dimension=1, tiled=True)
    gradient_base = lax.dot_general(
        cot, gathered, (((1,), (1,)), ((), ())), preferred_element_type=jnp.float32
    )
    return kv_base, gradient_base


def local(tokens, frozen_weight, cotangent, block_adapter_index, down_weight, up_weight):
    microbatch_list, token_block_rows, shard_width = tokens.shape
    kv_width = cotangent.shape[2]
    key_value_slice = kv_width // lax.axis_size("tp")
    row_total = microbatch_list * token_block_rows
    tok_matrix = tokens.reshape(row_total, shard_width)
    cot_matrix = cotangent.reshape(row_total, kv_width)
    adapter_number = down_weight.shape[0]
    rank_width = down_weight.shape[2]
    adapter_range = jnp.arange(adapter_number, dtype=jnp.int32)
    paired = (
        lax.axis_size("tp") == 2
        and lax.axis_size("fsdp") % 4 == 0
        and frozen_weight.shape[1] % LANES == 0
        and shard_width % (16 * LANES) == 0
    )
    base = paired_base if paired else plain_base
    frozen_key_value, frozen_input_gradient = base(tok_matrix, frozen_weight, cot_matrix)
    cot_slab = lax.dynamic_slice_in_dim(
        cotangent, lax.axis_index("tp") * key_value_slice, key_value_slice, 2
    )
    fsdp_count = lax.axis_size("fsdp")
    per_dev = token_block_rows // BLOCK
    dest_ids = (
        block_adapter_index.reshape(microbatch_list, fsdp_count, per_dev)
        .transpose(1, 0, 2)
        .reshape(fsdp_count, microbatch_list * per_dev)
    )
    down_send = jnp.take(down_weight, dest_ids, axis=0).transpose(0, 1, 3, 2)
    up_send = jnp.take(up_weight, dest_ids, axis=0)
    down_mine, up_mine = (
        lax.all_to_all(down_send, "fsdp", split_axis=0, concat_axis=3, tiled=True),
        lax.all_to_all(up_send, "fsdp", split_axis=0, concat_axis=3, tiled=True),
    )
    down_mine = down_mine.reshape(microbatch_list, per_dev, rank_width, shard_width)
    up_mine = up_mine.reshape(microbatch_list, per_dev, rank_width, key_value_slice)
    tok_blocks = tokens.reshape(microbatch_list, per_dev, BLOCK, shard_width)
    gradient_blocks = cot_slab.reshape(microbatch_list, per_dev, BLOCK, key_value_slice)
    low_part = jnp.einsum(
        "mnbc,mnrc->mnbr", tok_blocks, down_mine, preferred_element_type=jnp.float32
    )
    partial_input_gradient = adapter_scale * jnp.einsum(
        "fsvj,fsyj->fsvy", gradient_blocks, up_mine, preferred_element_type=jnp.float32
    )
    low_sum, back_sum = lax.psum((low_part, partial_input_gradient), "tp")
    low_rank = low_sum.astype(jnp.bfloat16)
    rank_gradient = back_sum.astype(jnp.bfloat16)
    adapter_key_value = (
        adapter_scale
        * jnp.einsum("elui,elis->elus", low_rank, up_mine, preferred_element_type=jnp.float32)
    ).astype(jnp.bfloat16)
    adapter_input_gradient = jnp.einsum(
        "mnbr,mnrc->mnbc", rank_gradient, down_mine, preferred_element_type=jnp.float32
    ).astype(jnp.bfloat16)
    adapter_key_value = adapter_key_value.reshape(
        microbatch_list, token_block_rows, key_value_slice
    )
    adapter_input_gradient = adapter_input_gradient.reshape(
        microbatch_list, token_block_rows, shard_width
    )
    down_tiles = jnp.einsum(
        "mnbc,mnbr->mnrc", tok_blocks, rank_gradient, preferred_element_type=jnp.float32
    )
    up_weight_tiles = adapter_scale * jnp.einsum(
        "puai,puac->puic", low_rank, gradient_blocks, preferred_element_type=jnp.float32
    )
    down_tiles = down_tiles.reshape(microbatch_list * per_dev, rank_width, shard_width)
    up_weight_tiles = up_weight_tiles.reshape(
        microbatch_list * per_dev, rank_width, key_value_slice
    )
    down_owned, up_owned = (
        lax.all_to_all(
            down_tiles.astype(jnp.bfloat16), "fsdp", split_axis=2, concat_axis=0, tiled=True
        ).astype(down_tiles.dtype),
        lax.all_to_all(
            up_weight_tiles.astype(jnp.bfloat16), "fsdp", split_axis=2, concat_axis=0, tiled=True
        ).astype(up_weight_tiles.dtype),
    )
    owned_ids = dest_ids.reshape(-1)
    adapter_selector = (owned_ids[:, None] == adapter_range[None, :]).astype(jnp.float32)
    grad_down = (
        selected_sum(adapter_selector, down_owned)
        .reshape(adapter_number, rank_width, down_weight.shape[1])
        .transpose(0, 2, 1)
    )
    up_weight_gradient = selected_sum(adapter_selector, up_owned).reshape(up_weight.shape)
    key_value_output = (
        frozen_key_value.reshape(microbatch_list, token_block_rows, key_value_slice)
        + adapter_key_value.astype(jnp.float32)
    ).astype(jnp.bfloat16)
    input_gradient = (
        frozen_input_gradient.reshape(microbatch_list, token_block_rows, shard_width)
        + adapter_input_gradient.astype(jnp.float32)
    ).astype(jnp.bfloat16)
    return (key_value_output, input_gradient, grad_down, up_weight_gradient)


def solution(mesh):
    return jax.shard_map(
        local,
        mesh=mesh,
        in_specs=(
            P(None, "fsdp", "tp"),
            P("tp", "fsdp"),
            P(None, "fsdp", None),
            P(),
            P(None, ("tp", "fsdp"), None),
            P(None, None, ("tp", "fsdp")),
        ),
        out_specs=(
            P(None, "fsdp", "tp"),
            P(None, "fsdp", "tp"),
            P(None, ("tp", "fsdp"), None),
            P(None, None, ("tp", "fsdp")),
        ),
        check_vma=False,
    )
```

```python
import functools

import jax
import jax.numpy as jnp
from jax import lax
from jax.experimental import pallas as pl
from jax.experimental.pallas import tpu as pltpu
from jax.sharding import PartitionSpec as P

BLOCK = 128
LANES = 128

adapter_scale = 2.0


ANYWHERE = pl.BlockSpec(memory_space=pl.ANY)
VMEM = pl.BlockSpec(memory_space=pltpu.VMEM)
SMEM = pl.BlockSpec(memory_space=pltpu.SMEM)
LIMIT = pltpu.CompilerParams(vmem_limit_bytes=56 * 1024 * 1024)

ROW_ROW = (((1,), (1,)), ((), ()))


def cost(flops, moved):
    return pl.CostEstimate(flops=flops, bytes_accessed=moved, transcendentals=0)


def dot(left, right, dims=(((1,), (0,)), ((), ()))):
    return lax.dot_general(left, right, dims, preferred_element_type=jnp.float32)


def one_hot(ids, count):
    lane = lax.broadcasted_iota(jnp.int32, (ids.shape[0], count), 1)
    return jnp.where(lane == ids, 1.0, 0.0).astype(jnp.bfloat16)


def pick(flag, first, second):
    return jnp.where(flag, first, second)


def send(value, axis, count, route):
    return lax.ppermute(value, axis, [(i, route(i)) for i in range(count)])


def chunk_kernel(plan, has_kv, has_out, last, start, half, *refs):
    refs = list(refs)
    take = lambda n: [refs.pop(0) for _ in range(n)]
    (place,) = take(1)
    arrays = take(max(array for array, _ in plan) + 1)
    tok_own, tok_pair, cot_own, cot_pair, back, down = take(6)
    (kv_in,) = take(1) if has_kv else (None,)
    if has_out:
        take(1)
    out, ig_pair = take(2)
    kv_out = take(2) if last else take(1)
    weight, tok, cot, factors, finished, kv, sems, kv_sems = refs
    rows = tok_own.shape[0]
    depth, total = weight.shape
    width = total // len(plan)
    x, core = place[len(plan)], place[len(plan) + 1]
    base = pl.multiple_of(x * half + start, LANES)
    column = lambda i: pl.multiple_of(place[i] * width, width)
    make = pltpu.make_async_copy
    count = len(plan)
    block_copies, kv_ins, kv_outs = [], [], []
    for i, (array, offset) in enumerate(plan):
        block_copies.append(
            make(
                arrays[array].at[pl.ds(offset, depth), :],
                weight.at[:, pl.ds(column(i), width)],
                sems.at[i],
            )
        )
        if has_kv:
            kv_ins.append(
                make(
                    kv_in.at[:, pl.ds(column(i), width)],
                    kv.at[:, pl.ds(column(i), width)],
                    kv_sems.at[i],
                )
            )
        if not last:
            kv_outs.append(
                make(
                    kv.at[:, pl.ds(column(i), width)],
                    kv_out[0].at[:, pl.ds(column(i), width)],
                    kv_sems.at[count + i],
                )
            )
    tok_copies = [
        make(tok_own.at[:, pl.ds(start, depth)], tok.at[pl.ds(0, rows), :], sems.at[count]),
        make(tok_pair.at[:, pl.ds(start, depth)], tok.at[pl.ds(rows, rows), :], sems.at[count + 1]),
    ]
    cot_copies = [
        make(cot_own, cot.at[pl.ds(0, rows), :], sems.at[count + 2]),
        make(cot_pair, cot.at[pl.ds(rows, rows), :], sems.at[count + 3]),
        make(down.at[:, :, pl.ds(base, depth)], factors, sems.at[count + 4]),
    ]
    for copy in tok_copies:
        copy.start()
    for i in range(count):
        block_copies[i].start()
        if has_kv:
            kv_ins[i].start()
    for copy in cot_copies:
        copy.start()
    for copy in tok_copies:
        copy.wait()
    for i in range(count):
        block_copies[i].wait()
        at = pl.ds(column(i), width)
        part = dot(tok[...], weight[:, at])
        if has_kv:
            kv_ins[i].wait()
            part = part + kv[:, at]
        if last:
            keep, other = kv_out
            columns = keep.shape[1]
            within = lax.rem(place[i] * width, columns)
            side = lax.div(place[i] * width, columns)
            slot = pl.ds(pl.multiple_of(within, width), width)

            @pl.when(side == core)
            def _():
                keep[:, slot] = part

            @pl.when(side != core)
            def _():
                other[:, slot] = part.astype(other.dtype)

        else:
            kv[:, at] = part
            kv_outs[i].start()
    for copy in cot_copies:
        copy.wait()
    tile = min(2 * LANES, depth)
    blocks = back.shape[0] // BLOCK

    @pl.loop(0, depth // tile)
    def _(step):
        at = pl.multiple_of(step * tile, tile)
        part = dot(cot[...], weight[pl.ds(at, tile), :], ROW_ROW)
        ig_pair[:, pl.ds(at, tile)] = part[rows:].astype(ig_pair.dtype)
        for m in range(blocks):
            own = pl.ds(m * BLOCK, BLOCK)
            adapter = dot(back[own, :], factors[m, :, pl.ds(at, tile)])
            adapter = adapter.astype(jnp.bfloat16).astype(jnp.float32)
            both = part[m * BLOCK : (m + 1) * BLOCK] + adapter
            finished[own, pl.ds(at, tile)] = both.astype(finished.dtype)

    result = make(finished, out.at[:, pl.ds(base, depth)], sems.at[count + 5])
    result.start()
    for copy in kv_outs:
        copy.wait()
    result.wait()


def chunk_product(
    place, plan, arrays, tok_own, tok_pair, cot_own, cot_pair, back, down, kv, out, start, depth, last, name
):
    rows, half = tok_own.shape
    total = cot_own.shape[1]
    count = len(plan)
    ranks = down.shape[1]
    blocks = rows // BLOCK
    operands = [place, *arrays, tok_own, tok_pair, cot_own, cot_pair, back, down]
    specs = [SMEM] + [ANYWHERE] * (len(arrays) + 4) + [VMEM, ANYWHERE]
    aliases = {}
    if kv is not None:
        operands.append(kv)
        specs.append(ANYWHERE)
    if out is not None:
        aliases[len(operands)] = 0
        operands.append(out)
        specs.append(ANYWHERE)
    shapes = [
        jax.ShapeDtypeStruct((rows, 2 * half), jnp.bfloat16),
        jax.ShapeDtypeStruct((rows, depth), jnp.bfloat16),
    ]
    out_specs = [ANYWHERE, VMEM]
    if last:
        shapes.append(jax.ShapeDtypeStruct((2 * rows, total // 2), jnp.float32))
        shapes.append(jax.ShapeDtypeStruct((2 * rows, total // 2), jnp.bfloat16))
        out_specs += [VMEM, VMEM]
    else:
        shapes.append(jax.ShapeDtypeStruct((2 * rows, total), jnp.float32))
        out_specs.append(ANYWHERE)
    return pl.pallas_call(
        functools.partial(chunk_kernel, plan, kv is not None, out is not None, last, start, half),
        name=name,
        out_shape=tuple(shapes),
        in_specs=specs,
        out_specs=tuple(out_specs),
        input_output_aliases=aliases,
        scratch_shapes=[
            pltpu.VMEM((depth, total), jnp.bfloat16),
            pltpu.VMEM((2 * rows, depth), jnp.bfloat16),
            pltpu.VMEM((2 * rows, total), jnp.bfloat16),
            pltpu.VMEM((blocks, ranks, depth), jnp.bfloat16),
            pltpu.VMEM((rows, depth), jnp.bfloat16),
            pltpu.VMEM((2 * rows, total), jnp.float32),
            pltpu.SemaphoreType.DMA((count + 6,)),
            pltpu.SemaphoreType.DMA((2 * count,)),
        ],
        cost_estimate=cost(8 * rows * depth * total, 2 * depth * total + 16 * rows * total),
        compiler_params=LIMIT,
    )(*operands)


def fetch_kernel(blocks, ids, ids_column, down, up, out, scratch, sems):
    devices, ranks = out.shape[0], down.shape[1]
    features = up.shape[0] // ranks
    copies = []
    for i in range(devices * blocks):
        copies.append(
            pltpu.make_async_copy(
                down.at[ids[i]],
                out.at[i // blocks, pl.ds(i % blocks * ranks, ranks), :],
                sems.at[i],
            )
        )
        copies[-1].start()
    count = up.shape[1]
    chosen = [one_hot(ids_column[pl.ds(m * devices, devices), :], count) for m in range(blocks)]
    for r in range(ranks):
        rows = up[pl.ds(r * features, features), :]
        scratch[:, r, :] = jnp.concatenate([dot(c, rows, ROW_ROW) for c in chosen], axis=1)
    lanes = blocks * features
    packed = scratch[...].astype(out.dtype)
    out[:, pl.ds(blocks * ranks, ranks), pl.ds(0, lanes)] = packed
    rest = out.shape[2] - lanes
    out[:, pl.ds(blocks * ranks, ranks), pl.ds(lanes, rest)] = jnp.zeros(
        (devices, ranks, rest), out.dtype
    )
    for copy in copies:
        copy.wait()


def project_kernel(blocks, core_ref, got, tok, cot, down_out, up_out, part):
    devices, ranks = got.shape[0], part.shape[1]
    width = got.shape[2]
    columns = up_out.shape[2]
    features = columns // devices
    at = pl.ds(pl.multiple_of(core_ref[0] * columns, LANES), columns)
    for m in range(blocks):
        for d in range(devices):
            down_out[m, :, pl.ds(d * width, width)] = got[d, pl.ds(m * ranks, ranks), :]
        lane = pl.ds(m * features, features)
        row = pl.ds(blocks * ranks, ranks)
        for d in range(0, devices, 2):
            up_out[m, :, pl.ds(d * features, 2 * features)] = jnp.concatenate(
                [got[d, row, lane], got[d + 1, row, lane]], axis=1
            )
        own = pl.ds(m * BLOCK, BLOCK)
        part[m] = dot(down_out[m], tok[own, :], ROW_ROW)
        part[blocks + m] = adapter_scale * dot(up_out[m], cot[own, at], ROW_ROW)


def tile_kernel(blocks, core_ref, part, other, tok, cot, out, low_out, back_out):
    devices, ranks, width = out.shape[0], part.shape[1], out.shape[2]
    columns = cot.shape[1] // 2
    features = columns // devices
    at = pl.ds(pl.multiple_of(core_ref[0] * columns, LANES), columns)
    summed = part[...] + other[...]
    ups = []
    for m in range(blocks):
        own = pl.ds(m * BLOCK, BLOCK)
        low = summed[m].astype(jnp.bfloat16)
        back = summed[blocks + m].astype(jnp.bfloat16)
        low_out[own, :] = jnp.transpose(summed[m]).astype(jnp.bfloat16)
        back_out[own, :] = jnp.transpose(summed[blocks + m]).astype(jnp.bfloat16)
        for d in range(devices):
            piece = dot(back, tok[own, pl.ds(d * width, width)])
            out[d, pl.ds(m * ranks, ranks), :] = piece.astype(out.dtype)
        ups.append(adapter_scale * dot(low, cot[own, at]))
    lanes = blocks * features
    for d in range(devices):
        piece = jnp.concatenate([u[:, d * features : (d + 1) * features] for u in ups], axis=1)
        out[d, pl.ds(blocks * ranks, ranks), pl.ds(0, lanes)] = piece.astype(out.dtype)
    rest = width - lanes
    out[:, pl.ds(blocks * ranks, ranks), pl.ds(lanes, rest)] = jnp.zeros(
        (devices, ranks, rest), out.dtype
    )


def spread_kernel(blocks, ids, ids_column, got, down_out, up_out, scratch):
    step = pl.program_id(0)
    many, ranks = down_out.shape[0], down_out.shape[1]
    devices = got.shape[0]
    down_out[...] = jnp.zeros(down_out.shape, down_out.dtype)
    for i in range(devices * blocks):
        where = ids[i] - step * many

        @pl.when((where >= 0) & (where < many))
        def _():
            tile = got[i // blocks, pl.ds(i % blocks * ranks, ranks), :].astype(jnp.float32)
            down_out[where] = down_out[where] + tile

    @pl.when(step == 0)
    def _():
        count = up_out.shape[1]
        features = up_out.shape[0] // ranks
        scratch[...] = got[:, pl.ds(blocks * ranks, ranks), pl.ds(0, blocks * features)].astype(
            jnp.float32
        )
        chosen = [one_hot(ids_column[pl.ds(m * devices, devices), :], count) for m in range(blocks)]
        for r in range(ranks):
            turned = jnp.transpose(scratch[:, r, :]).astype(jnp.bfloat16)
            total = 0.0
            for m in range(blocks):
                total = total + dot(turned[m * features : (m + 1) * features], chosen[m])
            up_out[pl.ds(r * features, features), :] = total


def kv_pair_kernel(keep, got, out):
    rows = out.shape[0]
    lower = pl.ds(rows, rows)
    out[...] = (keep[lower, :] + got[lower, :].astype(jnp.float32)).astype(out.dtype)


def kv_kernel(keep, core_got, pair_got, low, up, out):
    rows = out.shape[0]
    for m in range(rows // BLOCK):
        own = pl.ds(m * BLOCK, BLOCK)
        base = keep[own, :] + core_got[own, :].astype(jnp.float32)
        base = base + pair_got[own, :].astype(jnp.float32)
        adapter = adapter_scale * dot(low[own, :], up[m])
        adapter = adapter.astype(jnp.bfloat16).astype(jnp.float32)
        out[own, :] = (base + adapter).astype(out.dtype)


def rest_kernel(starts, half, *refs):
    count = len(starts)
    place, got, back, down, _, out = refs[0], refs[1 : 1 + count], *refs[1 + count : 5 + count]
    finished, factors, sems = refs[5 + count :]
    x = place[0]
    base = pl.multiple_of((1 - x) * half, LANES)
    load = pltpu.make_async_copy(down.at[:, :, pl.ds(base, half)], factors, sems.at[count])
    load.start()
    load.wait()
    copies = []
    for i, start in enumerate(starts):
        depth = got[i].shape[1]
        at = pl.ds(start, depth)
        for m in range(factors.shape[0]):
            own = pl.ds(m * BLOCK, BLOCK)
            adapter = dot(back[own, :], factors[m, :, at]).astype(jnp.bfloat16)
            both = got[i][own, :].astype(jnp.float32) + adapter.astype(jnp.float32)
            finished[own, at] = both.astype(finished.dtype)
        copies.append(
            pltpu.make_async_copy(
                finished.at[:, at],
                out.at[:, pl.ds(pl.multiple_of(base + start, LANES), depth)],
                sems.at[i],
            )
        )
        copies[-1].start()
    for copy in copies:
        copy.wait()


def paired(tokens, frozen_weight, cotangent, block_adapter_index, down_weight, up_weight):
    batches, batch_rows, shard = tokens.shape
    total = cotangent.shape[2]
    columns = total // 2
    rows = batches * batch_rows
    half = shard // 2
    tok = tokens.reshape(rows, shard)
    cot = cotangent.reshape(rows, total)
    adapters, down_rows, ranks = down_weight.shape
    features = up_weight.shape[2]
    per_device = batch_rows // BLOCK
    blocks = batches * per_device
    count = lax.axis_size("fsdp")
    layers = count // 4
    index = lax.axis_index("fsdp")
    core = lax.axis_index("tp")
    x, y, z = index % 2, (index // 2) % 2, index // 4
    low = x == 0
    left = core == 0
    bf16, f32 = jnp.bfloat16, jnp.float32
    shape = jax.ShapeDtypeStruct

    x_send = lambda v: send(v, "fsdp", count, lambda i: i ^ 1)
    y_send = lambda v: send(v, "fsdp", count, lambda i: i ^ 2)
    z_send = lambda v: send(v, "fsdp", count, lambda i: (i + 4) % count)
    core_send = lambda v: send(v, "tp", 2, lambda i: i ^ 1)

    unit = half // 8
    chunks = ((0, 4 * unit, "zy"), (4 * unit, 3 * unit, "zy"), (7 * unit, unit, "yz"))
    pair_blocks = []
    for start, depth, _ in chunks:
        first = frozen_weight[start : start + depth]
        second = frozen_weight[half + start : half + start + depth]
        mine = pick(low, first, second)
        got = x_send(pick(low, second, first))
        pair_blocks.append(
            jnp.concatenate([pick(low, mine, got), pick(low, got, mine)], axis=1)
        )
    tok_own = pick(low, tok[:, :half], tok[:, half:])
    tok_pair = x_send(pick(low, tok[:, half:], tok[:, :half]))
    cot_part = x_send(pick(left, cot[:, :columns], cot[:, columns:]))
    cot_rest = core_send(cot_part)
    cot_pair = jnp.concatenate(
        [pick(left, cot_part, cot_rest), pick(left, cot_rest, cot_part)], axis=1
    )

    ids = (
        block_adapter_index.reshape(batches, count, per_device)
        .transpose(1, 0, 2)
        .reshape(count, blocks)
    )
    id_list = ids.reshape(-1)
    id_column = ids.T.reshape(-1, 1)
    exchange = lambda v: lax.all_to_all(v, "fsdp", split_axis=0, concat_axis=0, tiled=True)
    packet = shape((count, (blocks + 1) * ranks, down_rows), bf16)
    packet_bytes = 2 * count * (blocks + 1) * ranks * down_rows
    parcel = pl.pallas_call(
        functools.partial(fetch_kernel, blocks),
        name="fetch",
        out_shape=packet,
        in_specs=[SMEM, VMEM, ANYWHERE, VMEM],
        out_specs=VMEM,
        scratch_shapes=[
            pltpu.VMEM((count, ranks, blocks * features), f32),
            pltpu.SemaphoreType.DMA((count * blocks,)),
        ],
        cost_estimate=cost(0, 4 * packet_bytes),
        compiler_params=LIMIT,
    )(
        id_list,
        id_column,
        down_weight.transpose(0, 2, 1),
        up_weight.transpose(1, 2, 0).reshape(ranks * features, adapters),
    )
    arrived = exchange(parcel)
    core_place = core.astype(jnp.int32).reshape(1)
    down_mine, up_mine, part = pl.pallas_call(
        functools.partial(project_kernel, blocks),
        name="project",
        out_shape=(
            shape((blocks, ranks, shard), bf16),
            shape((blocks, ranks, columns), bf16),
            shape((2 * blocks, ranks, BLOCK), f32),
        ),
        in_specs=[SMEM, VMEM, VMEM, VMEM],
        out_specs=(VMEM, VMEM, VMEM),
        cost_estimate=cost(2 * rows * ranks * (shard + columns), 2 * rows * (shard + total)),
        compiler_params=LIMIT,
    )(core_place, arrived, tok, cot)
    other = core_send(part)
    tiles, low_rank, back_rank = pl.pallas_call(
        functools.partial(tile_kernel, blocks),
        name="tiles",
        out_shape=(packet, shape((rows, ranks), bf16), shape((rows, ranks), bf16)),
        in_specs=[SMEM, VMEM, VMEM, VMEM, VMEM],
        out_specs=(VMEM, VMEM, VMEM),
        cost_estimate=cost(2 * rows * ranks * (shard + columns), 2 * rows * (shard + total)),
        compiler_params=LIMIT,
    )(core_place, part, other, tok, cot)
    owned = exchange(tiles)
    many = adapters // 8
    grad_down, grad_up = pl.pallas_call(
        functools.partial(spread_kernel, blocks),
        name="spread",
        grid=(adapters // many,),
        out_shape=(
            shape((adapters, ranks, down_rows), f32),
            shape((ranks * features, adapters), f32),
        ),
        in_specs=[SMEM, VMEM, VMEM],
        out_specs=(
            pl.BlockSpec((many, ranks, down_rows), lambda i: (i, 0, 0)),
            pl.BlockSpec((ranks * features, adapters), lambda i: (0, 0)),
        ),
        scratch_shapes=[pltpu.VMEM((count, ranks, blocks * features), f32)],
        cost_estimate=cost(0, 4 * adapters * ranks * (down_rows + features)),
        compiler_params=LIMIT,
    )(id_list, id_column, owned)

    kv = out = None
    got_pieces = []
    for (start, depth, order), block in zip(chunks, pair_blocks):
        arrays, plan, places = [], [], []
        held = block
        if order == "yz":
            held = jnp.concatenate([block, y_send(block)], axis=0)
        for step in range(layers):
            if step:
                held = z_send(held)
            layer = (z - step) % layers
            places += [layer * 2 + y, layer * 2 + 1 - y]
            if order == "yz":
                plan += [(len(arrays), 0), (len(arrays), depth)]
                arrays.append(held)
            else:
                plan += [(len(arrays), 0), (len(arrays) + 1, 0)]
                arrays += [held, y_send(held)]
        last = start + depth == half
        results = chunk_product(
            jnp.stack(places + [x, core]).astype(jnp.int32),
            tuple(plan),
            arrays,
            tok_own,
            tok_pair,
            cot,
            cot_pair,
            back_rank,
            down_mine,
            kv,
            out,
            start,
            depth,
            last,
            f"base_{start}",
        )
        out, pair = results[:2]
        kv = results[2]
        got_pieces.append(x_send(pair))
    keep, other_columns = results[2:]
    core_got = core_send(other_columns)
    pair_sum = pl.pallas_call(
        kv_pair_kernel,
        name="kv_pair",
        out_shape=shape((rows, columns), bf16),
        in_specs=[VMEM, VMEM],
        out_specs=VMEM,
        cost_estimate=cost(0, 12 * rows * columns),
        compiler_params=LIMIT,
    )(keep, core_got)
    pair_got = x_send(pair_sum)
    key_value = pl.pallas_call(
        kv_kernel,
        name="kv_end",
        out_shape=shape((rows, columns), bf16),
        in_specs=[VMEM] * 5,
        out_specs=VMEM,
        cost_estimate=cost(2 * rows * ranks * columns, 12 * rows * columns),
        compiler_params=LIMIT,
    )(keep, core_got, pair_got, low_rank, up_mine)
    starts = tuple(start for start, _, _ in chunks)
    out = pl.pallas_call(
        functools.partial(rest_kernel, starts, half),
        name="rest",
        out_shape=shape((rows, shard), bf16),
        in_specs=[SMEM] + [VMEM] * (len(starts) + 1) + [ANYWHERE, ANYWHERE],
        out_specs=ANYWHERE,
        input_output_aliases={len(starts) + 3: 0},
        scratch_shapes=[
            pltpu.VMEM((rows, half), bf16),
            pltpu.VMEM((blocks, ranks, half), bf16),
            pltpu.SemaphoreType.DMA((len(starts) + 1,)),
        ],
        cost_estimate=cost(2 * rows * ranks * half, 4 * rows * half),
        compiler_params=LIMIT,
    )(x.astype(jnp.int32).reshape(1), *got_pieces, back_rank, down_mine, out)
    return (
        key_value.reshape(batches, batch_rows, columns),
        out.reshape(batches, batch_rows, shard),
        grad_down.transpose(0, 2, 1),
        grad_up.reshape(ranks, features, adapters).transpose(2, 0, 1),
    )


def selected_sum(adapter_selector, tiles):
    flat = tiles.reshape(tiles.shape[0], -1)
    return lax.dot_general(
        adapter_selector,
        flat,
        (((0,), (0,)), ((), ())),
        precision=lax.Precision.HIGHEST,
        preferred_element_type=jnp.float32,
    )


def plain(tokens, frozen_weight, cotangent, block_adapter_index, down_weight, up_weight):
    microbatch_list, token_block_rows, shard_width = tokens.shape
    kv_width = cotangent.shape[2]
    key_value_slice = kv_width // lax.axis_size("tp")
    row_total = microbatch_list * token_block_rows
    tok_matrix = tokens.reshape(row_total, shard_width)
    cot_matrix = cotangent.reshape(row_total, kv_width)
    adapter_number = down_weight.shape[0]
    rank_width = down_weight.shape[2]
    adapter_range = jnp.arange(adapter_number, dtype=jnp.int32)
    gathered = lax.all_gather(frozen_weight, "fsdp", axis=1, tiled=True)
    kv_partial = jnp.dot(tok_matrix, gathered, preferred_element_type=jnp.float32)
    frozen_key_value = lax.psum_scatter(kv_partial, "tp", scatter_dimension=1, tiled=True)
    frozen_input_gradient = lax.dot_general(
        cot_matrix, gathered, (((1,), (1,)), ((), ())), preferred_element_type=jnp.float32
    )
    cot_slab = lax.dynamic_slice_in_dim(
        cotangent, lax.axis_index("tp") * key_value_slice, key_value_slice, 2
    )
    fsdp_count = lax.axis_size("fsdp")
    per_dev = token_block_rows // BLOCK
    dest_ids = (
        block_adapter_index.reshape(microbatch_list, fsdp_count, per_dev)
        .transpose(1, 0, 2)
        .reshape(fsdp_count, microbatch_list * per_dev)
    )
    down_send = jnp.take(down_weight, dest_ids, axis=0).transpose(0, 1, 3, 2)
    up_send = jnp.take(up_weight, dest_ids, axis=0)
    down_mine, up_mine = (
        lax.all_to_all(down_send, "fsdp", split_axis=0, concat_axis=3, tiled=True),
        lax.all_to_all(up_send, "fsdp", split_axis=0, concat_axis=3, tiled=True),
    )
    down_mine = down_mine.reshape(microbatch_list, per_dev, rank_width, shard_width)
    up_mine = up_mine.reshape(microbatch_list, per_dev, rank_width, key_value_slice)
    tok_blocks = tokens.reshape(microbatch_list, per_dev, BLOCK, shard_width)
    gradient_blocks = cot_slab.reshape(microbatch_list, per_dev, BLOCK, key_value_slice)
    low_part = jnp.einsum(
        "mnbc,mnrc->mnbr", tok_blocks, down_mine, preferred_element_type=jnp.float32
    )
    partial_input_gradient = adapter_scale * jnp.einsum(
        "fsvj,fsyj->fsvy", gradient_blocks, up_mine, preferred_element_type=jnp.float32
    )
    low_sum, back_sum = lax.psum((low_part, partial_input_gradient), "tp")
    low_rank = low_sum.astype(jnp.bfloat16)
    rank_gradient = back_sum.astype(jnp.bfloat16)
    adapter_key_value = (
        adapter_scale
        * jnp.einsum("elui,elis->elus", low_rank, up_mine, preferred_element_type=jnp.float32)
    ).astype(jnp.bfloat16)
    adapter_input_gradient = jnp.einsum(
        "mnbr,mnrc->mnbc", rank_gradient, down_mine, preferred_element_type=jnp.float32
    ).astype(jnp.bfloat16)
    adapter_key_value = adapter_key_value.reshape(
        microbatch_list, token_block_rows, key_value_slice
    )
    adapter_input_gradient = adapter_input_gradient.reshape(
        microbatch_list, token_block_rows, shard_width
    )
    down_tiles = jnp.einsum(
        "mnbc,mnbr->mnrc", tok_blocks, rank_gradient, preferred_element_type=jnp.float32
    )
    up_weight_tiles = adapter_scale * jnp.einsum(
        "puai,puac->puic", low_rank, gradient_blocks, preferred_element_type=jnp.float32
    )
    down_tiles = down_tiles.reshape(microbatch_list * per_dev, rank_width, shard_width)
    up_weight_tiles = up_weight_tiles.reshape(
        microbatch_list * per_dev, rank_width, key_value_slice
    )
    down_owned, up_owned = (
        lax.all_to_all(
            down_tiles.astype(jnp.bfloat16), "fsdp", split_axis=2, concat_axis=0, tiled=True
        ).astype(down_tiles.dtype),
        lax.all_to_all(
            up_weight_tiles.astype(jnp.bfloat16), "fsdp", split_axis=2, concat_axis=0, tiled=True
        ).astype(up_weight_tiles.dtype),
    )
    owned_ids = dest_ids.reshape(-1)
    adapter_selector = (owned_ids[:, None] == adapter_range[None, :]).astype(jnp.float32)
    grad_down = (
        selected_sum(adapter_selector, down_owned)
        .reshape(adapter_number, rank_width, down_weight.shape[1])
        .transpose(0, 2, 1)
    )
    up_weight_gradient = selected_sum(adapter_selector, up_owned).reshape(up_weight.shape)
    key_value_output = (
        frozen_key_value.reshape(microbatch_list, token_block_rows, key_value_slice)
        + adapter_key_value.astype(jnp.float32)
    ).astype(jnp.bfloat16)
    input_gradient = (
        frozen_input_gradient.reshape(microbatch_list, token_block_rows, shard_width)
        + adapter_input_gradient.astype(jnp.float32)
    ).astype(jnp.bfloat16)
    return (key_value_output, input_gradient, grad_down, up_weight_gradient)


def local(tokens, frozen_weight, cotangent, block_adapter_index, down_weight, up_weight):
    batches, batch_rows, shard = tokens.shape
    blocks = batches * (batch_rows // BLOCK)
    features = up_weight.shape[2]
    fits = (
        lax.axis_size("tp") == 2
        and lax.axis_size("fsdp") % 4 == 0
        and frozen_weight.shape[1] % LANES == 0
        and shard % (16 * 2 * LANES) == 0
        and blocks * features == LANES
        and 2 * features == LANES
        and down_weight.shape[1] > LANES
        and down_weight.shape[0] % (8 * LANES // 2) == 0
    )
    body = paired if fits else plain
    return body(tokens, frozen_weight, cotangent, block_adapter_index, down_weight, up_weight)


def solution(mesh):
    return jax.shard_map(
        local,
        mesh=mesh,
        in_specs=(
            P(None, "fsdp", "tp"),
            P("tp", "fsdp"),
            P(None, "fsdp", None),
            P(),
            P(None, ("tp", "fsdp"), None),
            P(None, None, ("tp", "fsdp")),
        ),
        out_specs=(
            P(None, "fsdp", "tp"),
            P(None, "fsdp", "tp"),
            P(None, ("tp", "fsdp"), None),
            P(None, None, ("tp", "fsdp")),
        ),
        check_vma=False,
    )
```

```python
import functools

import jax
import jax.numpy as jnp
from jax import lax
from jax.experimental import pallas as pl
from jax.experimental.pallas import tpu as pltpu
from jax.sharding import PartitionSpec as P


BLOCK = 128
LANES = 128

adapter_scale = 2.0


ANYWHERE = pl.BlockSpec(memory_space=pl.ANY)
VMEM = pl.BlockSpec(memory_space=pltpu.VMEM)
SMEM = pl.BlockSpec(memory_space=pltpu.SMEM)
LIMIT = pltpu.CompilerParams(vmem_limit_bytes=34 * 1024 * 1024)

ROW_ROW = (((1,), (1,)), ((), ()))


def cost(flops, moved):
    return pl.CostEstimate(flops=flops, bytes_accessed=moved, transcendentals=0)


def dot(left, right, dims=(((1,), (0,)), ((), ()))):
    return lax.dot_general(left, right, dims, preferred_element_type=jnp.float32)


def one_hot(ids, count):
    lane = lax.broadcasted_iota(jnp.int32, (ids.shape[0], count), 1)
    return jnp.where(lane == ids, 1.0, 0.0).astype(jnp.bfloat16)


def send(value, axis, count, route):
    return lax.ppermute(value, axis, [(i, route(i)) for i in range(count)])


def first_kernel(start, half, place, weight, theirs, sem):
    other = pl.multiple_of((1 - place[0]) * half + start, LANES)
    copy = pltpu.make_async_copy(weight.at[pl.ds(other, theirs.shape[0]), :], theirs, sem)
    copy.start()
    copy.wait()


def prep_kernel(start, place, weight, tok, cot, mine, theirs, tok_out, cot_out, sems):
    half = mine.shape[0]
    columns = cot_out.shape[1]
    x, core = place[0], place[1]
    own = pl.multiple_of(x * half, LANES)
    other = pl.multiple_of((1 - x) * half, LANES)
    side = pl.multiple_of(core * columns, LANES)
    copies = [
        pltpu.make_async_copy(
            weight.at[pl.ds(other + start, half - start), :], theirs, sems.at[0]
        ),
        pltpu.make_async_copy(weight.at[pl.ds(own, half), :], mine, sems.at[1]),
        pltpu.make_async_copy(tok.at[:, pl.ds(other, half)], tok_out, sems.at[2]),
        pltpu.make_async_copy(cot.at[:, pl.ds(side, columns)], cot_out, sems.at[3]),
    ]
    for copy in copies:
        copy.start()
    for copy in copies:
        copy.wait()


def pair_kernel(start, place, mine, theirs, out):
    depth, width = theirs.shape
    own = pl.ds(pl.multiple_of(place[0] * width, LANES), width)
    other = pl.ds(pl.multiple_of((1 - place[0]) * width, LANES), width)
    out[:, own] = mine[pl.ds(start, depth), :]
    out[:, other] = theirs[...]


WHOLE, MINE, THEIRS = 0, 1, 2


def chunk_kernel(plan, array_count, has_kv, last, start, half, *refs):
    refs = list(refs)
    take = lambda n: [refs.pop(0) for _ in range(n)]
    (place,) = take(1)
    arrays = take(array_count)
    tok_all, tok_pair, cot_own, cot_part, cot_rest, back, down = take(7)
    kv_in, _ = take(2) if has_kv else (None, None)
    out, ig_pair = take(2)
    kv_out = take(2) if last else take(1)
    weight, tok, cot, finished, sem = refs[:5]
    rows = tok_all.shape[0]
    depth, total = weight.shape
    count = len(plan)
    width = total // count
    columns = cot_part.shape[1]
    x, core = place[count], place[count + 1]
    base = pl.multiple_of(x * half + start, LANES)
    lower = pl.ds(rows, rows)
    tok[pl.ds(0, rows), :] = tok_all[:, pl.ds(base, depth)]
    tok[lower, :] = tok_pair[:, pl.ds(start, depth)]
    for i, pieces in enumerate(plan):
        for array, offset, kind in pieces:
            wide = arrays[array].shape[1]
            shift = {WHOLE: 0, MINE: x * wide, THEIRS: (1 - x) * wide}[kind]
            target = pl.ds(pl.multiple_of(place[i] * width + shift, LANES), wide)
            weight[:, target] = arrays[array][pl.ds(offset, depth), :]
        at = pl.ds(pl.multiple_of(place[i] * width, LANES), width)
        part = dot(tok[...], weight[:, at])
        if has_kv:
            part = part + kv_in[:, at]
        if last:
            wide_kv, narrow_kv = refs[5:]
            slot = pl.ds(pl.multiple_of(lax.rem(place[i] * width, columns), LANES), width)
            where = lax.rem(lax.div(place[i] * width, columns) + core, 2)
            wide_kv[where, :, slot] = part
            narrow_kv[where, :, slot] = part.astype(narrow_kv.dtype)
        else:
            kv_out[0][:, at] = part
    if last:
        kv_out[0][...] = wide_kv[0]
        kv_out[1][...] = narrow_kv[1]
    cot[pl.ds(0, rows), :] = cot_own[...]
    cot[lower, pl.ds(pl.multiple_of(core * columns, LANES), columns)] = cot_part[...]
    cot[lower, pl.ds(pl.multiple_of((1 - core) * columns, LANES), columns)] = cot_rest[...]
    tile = min(2 * LANES, depth)
    blocks = back.shape[0] // BLOCK

    @pl.loop(0, depth // tile)
    def _(step):
        at = pl.multiple_of(step * tile, tile)
        wide = pl.ds(pl.multiple_of(base + step * tile, LANES), tile)
        part = dot(cot[...], weight[pl.ds(at, tile), :], ROW_ROW)
        ig_pair[:, pl.ds(at, tile)] = part[rows:].astype(ig_pair.dtype)
        for m in range(blocks):
            own = pl.ds(m * BLOCK, BLOCK)
            adapter = dot(back[own, :], down[m, :, wide])
            adapter = adapter.astype(jnp.bfloat16).astype(jnp.float32)
            both = part[m * BLOCK : (m + 1) * BLOCK] + adapter
            finished[own, pl.ds(at, tile)] = both.astype(finished.dtype)

    result = pltpu.make_async_copy(finished, out.at[:, pl.ds(base, depth)], sem)
    result.start()
    result.wait()


def chunk_product(
    place, plan, arrays, tok, tok_pair, cot, cot_part, cot_rest, back, down, kv, out, start, depth, last
):
    rows, half = tok_pair.shape
    total = cot.shape[1]
    operands = [place, *arrays, tok, tok_pair, cot, cot_part, cot_rest, back, down]
    specs = [SMEM] + [VMEM] * (len(arrays) + 7)
    aliases = {}
    if kv is not None:
        aliases[len(operands) + 1] = 0
        operands += [kv, out]
        specs += [VMEM, ANYWHERE]
    shapes = [
        jax.ShapeDtypeStruct((rows, 2 * half), jnp.bfloat16),
        jax.ShapeDtypeStruct((rows, depth), jnp.bfloat16),
    ]
    out_specs = [ANYWHERE, VMEM]
    if last:
        shapes.append(jax.ShapeDtypeStruct((2 * rows, total // 2), jnp.float32))
        shapes.append(jax.ShapeDtypeStruct((2 * rows, total // 2), jnp.bfloat16))
        out_specs += [VMEM, VMEM]
    else:
        shapes.append(jax.ShapeDtypeStruct((2 * rows, total), jnp.float32))
        out_specs.append(VMEM)
    return pl.pallas_call(
        functools.partial(chunk_kernel, plan, len(arrays), kv is not None, last, start, half),
        out_shape=tuple(shapes),
        in_specs=specs,
        out_specs=tuple(out_specs),
        input_output_aliases=aliases,
        scratch_shapes=[
            pltpu.VMEM((depth, total), jnp.bfloat16),
            pltpu.VMEM((2 * rows, depth), jnp.bfloat16),
            pltpu.VMEM((2 * rows, total), jnp.bfloat16),
            pltpu.VMEM((rows, depth), jnp.bfloat16),
            pltpu.SemaphoreType.DMA,
        ]
        + [pltpu.VMEM((2, 2 * rows, total // 2), kind) for kind in (jnp.float32, jnp.bfloat16) if last],
        cost_estimate=cost(8 * rows * depth * total, 2 * depth * total + 16 * rows * total),
        compiler_params=LIMIT,
    )(*operands)


def fetch_kernel(blocks, ids, ids_column, down, up, out, scratch, sems):
    devices, ranks = out.shape[0], down.shape[1]
    features = up.shape[0] // ranks
    copies = []
    for i in range(devices * blocks):
        copies.append(
            pltpu.make_async_copy(
                down.at[ids[i]],
                out.at[i // blocks, pl.ds(i % blocks * ranks, ranks), :],
                sems.at[i],
            )
        )
        copies[-1].start()
    count = up.shape[1]
    chosen = [one_hot(ids_column[pl.ds(m * devices, devices), :], count) for m in range(blocks)]
    for r in range(ranks):
        rows = up[pl.ds(r * features, features), :]
        scratch[:, r, :] = jnp.concatenate([dot(c, rows, ROW_ROW) for c in chosen], axis=1)
    lanes = blocks * features
    packed = scratch[...].astype(out.dtype)
    out[:, pl.ds(blocks * ranks, ranks), pl.ds(0, lanes)] = packed
    rest = out.shape[2] - lanes
    out[:, pl.ds(blocks * ranks, ranks), pl.ds(lanes, rest)] = jnp.zeros(
        (devices, ranks, rest), out.dtype
    )
    for copy in copies:
        copy.wait()


def project_kernel(blocks, core_ref, got, tok, cot, down_out, up_out, part):
    devices, ranks = got.shape[0], part.shape[1]
    width = got.shape[2]
    columns = up_out.shape[2]
    features = columns // devices
    at = pl.ds(pl.multiple_of(core_ref[0] * columns, LANES), columns)
    for m in range(blocks):
        for d in range(devices):
            down_out[m, :, pl.ds(d * width, width)] = got[d, pl.ds(m * ranks, ranks), :]
        lane = pl.ds(m * features, features)
        row = pl.ds(blocks * ranks, ranks)
        for d in range(0, devices, 2):
            up_out[m, :, pl.ds(d * features, 2 * features)] = jnp.concatenate(
                [got[d, row, lane], got[d + 1, row, lane]], axis=1
            )
        own = pl.ds(m * BLOCK, BLOCK)
        part[m] = dot(down_out[m], tok[own, :], ROW_ROW)
        part[blocks + m] = adapter_scale * dot(up_out[m], cot[own, at], ROW_ROW)


def tile_kernel(blocks, core_ref, part, other, tok, cot, out, low_out, back_out):
    devices, ranks, width = out.shape[0], part.shape[1], out.shape[2]
    columns = cot.shape[1] // 2
    features = columns // devices
    at = pl.ds(pl.multiple_of(core_ref[0] * columns, LANES), columns)
    summed = part[...] + other[...]
    ups = []
    for m in range(blocks):
        own = pl.ds(m * BLOCK, BLOCK)
        low = summed[m].astype(jnp.bfloat16)
        back = summed[blocks + m].astype(jnp.bfloat16)
        low_out[own, :] = jnp.transpose(summed[m]).astype(jnp.bfloat16)
        back_out[own, :] = jnp.transpose(summed[blocks + m]).astype(jnp.bfloat16)
        for d in range(devices):
            piece = dot(back, tok[own, pl.ds(d * width, width)])
            out[d, pl.ds(m * ranks, ranks), :] = piece.astype(out.dtype)
        ups.append(adapter_scale * dot(low, cot[own, at]))
    lanes = blocks * features
    for d in range(devices):
        piece = jnp.concatenate([u[:, d * features : (d + 1) * features] for u in ups], axis=1)
        out[d, pl.ds(blocks * ranks, ranks), pl.ds(0, lanes)] = piece.astype(out.dtype)
    rest = width - lanes
    out[:, pl.ds(blocks * ranks, ranks), pl.ds(lanes, rest)] = jnp.zeros(
        (devices, ranks, rest), out.dtype
    )


def spread_kernel(blocks, ids, ids_column, got, down_out, up_out, scratch):
    step = pl.program_id(0)
    many, ranks = down_out.shape[0], down_out.shape[1]
    devices = got.shape[0]
    down_out[...] = jnp.zeros(down_out.shape, down_out.dtype)
    for i in range(devices * blocks):
        where = ids[i] - step * many

        @pl.when((where >= 0) & (where < many))
        def _():
            tile = got[i // blocks, pl.ds(i % blocks * ranks, ranks), :].astype(jnp.float32)
            down_out[where] = down_out[where] + tile

    @pl.when(step == 0)
    def _():
        count = up_out.shape[1]
        features = up_out.shape[0] // ranks
        scratch[...] = got[:, pl.ds(blocks * ranks, ranks), pl.ds(0, blocks * features)].astype(
            jnp.float32
        )
        chosen = [one_hot(ids_column[pl.ds(m * devices, devices), :], count) for m in range(blocks)]
        for r in range(ranks):
            turned = jnp.transpose(scratch[:, r, :]).astype(jnp.bfloat16)
            total = 0.0
            for m in range(blocks):
                total = total + dot(turned[m * features : (m + 1) * features], chosen[m])
            up_out[pl.ds(r * features, features), :] = total


def kv_pair_kernel(keep, got, out):
    rows = out.shape[0]
    lower = pl.ds(rows, rows)
    out[...] = (keep[lower, :] + got[lower, :].astype(jnp.float32)).astype(out.dtype)


def kv_kernel(keep, core_got, pair_got, low, up, out):
    rows = out.shape[0]
    for m in range(rows // BLOCK):
        own = pl.ds(m * BLOCK, BLOCK)
        base = keep[own, :] + core_got[own, :].astype(jnp.float32)
        base = base + pair_got[own, :].astype(jnp.float32)
        adapter = adapter_scale * dot(low[own, :], up[m])
        adapter = adapter.astype(jnp.bfloat16).astype(jnp.float32)
        out[own, :] = (base + adapter).astype(out.dtype)


def rest_kernel(starts, half, *refs):
    count = len(starts)
    place, got, back, down, _, out = refs[0], refs[1 : 1 + count], *refs[1 + count : 5 + count]
    finished, factors, sems = refs[5 + count :]
    x = place[0]
    base = pl.multiple_of((1 - x) * half, LANES)
    load = pltpu.make_async_copy(down.at[:, :, pl.ds(base, half)], factors, sems.at[count])
    load.start()
    load.wait()
    copies = []
    for i, start in enumerate(starts):
        depth = got[i].shape[1]
        at = pl.ds(start, depth)
        for m in range(factors.shape[0]):
            own = pl.ds(m * BLOCK, BLOCK)
            adapter = dot(back[own, :], factors[m, :, at]).astype(jnp.bfloat16)
            both = got[i][own, :].astype(jnp.float32) + adapter.astype(jnp.float32)
            finished[own, at] = both.astype(finished.dtype)
        copies.append(
            pltpu.make_async_copy(
                finished.at[:, at],
                out.at[:, pl.ds(pl.multiple_of(base + start, LANES), depth)],
                sems.at[i],
            )
        )
        copies[-1].start()
    for copy in copies:
        copy.wait()


def paired(tokens, frozen_weight, cotangent, block_adapter_index, down_weight, up_weight):
    batches, batch_rows, shard = tokens.shape
    total = cotangent.shape[2]
    columns = total // 2
    rows = batches * batch_rows
    half = shard // 2
    tok = tokens.reshape(rows, shard)
    cot = cotangent.reshape(rows, total)
    adapters, down_rows, ranks = down_weight.shape
    features = up_weight.shape[2]
    per_device = batch_rows // BLOCK
    blocks = batches * per_device
    count = lax.axis_size("fsdp")
    layers = count // 4
    index = lax.axis_index("fsdp")
    core = lax.axis_index("tp")
    x, y, z = index % 2, (index // 2) % 2, index // 4
    bf16, f32 = jnp.bfloat16, jnp.float32
    shape = jax.ShapeDtypeStruct

    def move(axis, width, route, value):
        return send(value, axis, width, route)

    x_send = lambda v: move("fsdp", count, lambda i: i ^ 1, v)
    y_send = lambda v: move("fsdp", count, lambda i: i ^ 2, v)
    z_send = lambda v: move("fsdp", count, lambda i: (i + 4) % count, v)
    core_send = lambda v: move("tp", 2, lambda i: i ^ 1, v)

    chunks = ((0, half // 2), (half // 2, half // 2))
    block = frozen_weight.shape[1]
    here = jnp.stack([x, core]).astype(jnp.int32)
    split = chunks[1][0]
    theirs = [
        pl.pallas_call(
            functools.partial(first_kernel, 0, half),
            name="first",
            out_shape=shape((split, block), bf16),
            in_specs=[SMEM, ANYWHERE],
            out_specs=VMEM,
            scratch_shapes=[pltpu.SemaphoreType.DMA],
            cost_estimate=cost(0, 4 * split * block),
            compiler_params=LIMIT,
        )(here, frozen_weight)
    ]
    mine, later, tok_sent, cot_sent = pl.pallas_call(
        functools.partial(prep_kernel, split),
        name="prep",
        out_shape=(
            shape((half, block), bf16),
            shape((half - split, block), bf16),
            shape((rows, half), bf16),
            shape((rows, columns), bf16),
        ),
        in_specs=[SMEM, ANYWHERE, ANYWHERE, ANYWHERE],
        out_specs=(VMEM,) * 4,
        scratch_shapes=[pltpu.SemaphoreType.DMA((4,))],
        cost_estimate=cost(0, 4 * (2 * half * block + rows * (half + columns))),
        compiler_params=LIMIT,
    )(here, frozen_weight, tok, cot)
    theirs.append(later)
    mine_y = y_send(mine)
    tok_pair = x_send(tok_sent)
    cot_part = x_send(cot_sent)
    cot_rest = core_send(cot_part)
    held, theirs_y = [], []
    for c, (start, depth) in enumerate(chunks):
        got = x_send(theirs[c])
        held.append(
            pl.pallas_call(
                functools.partial(pair_kernel, start),
                out_shape=shape((depth, 2 * block), bf16),
                in_specs=[SMEM, VMEM, VMEM],
                out_specs=VMEM,
                cost_estimate=cost(0, 8 * depth * block),
                compiler_params=LIMIT,
            )(here, mine, got)
        )
        theirs_y.append(y_send(got))

    ids = (
        block_adapter_index.reshape(batches, count, per_device)
        .transpose(1, 0, 2)
        .reshape(count, blocks)
    )
    id_list = ids.reshape(-1)
    id_column = ids.T.reshape(-1, 1)

    def exchange(value):
        return lax.all_to_all(value, "fsdp", split_axis=0, concat_axis=0, tiled=True)

    packet = shape((count, (blocks + 1) * ranks, down_rows), bf16)
    packet_bytes = 2 * count * (blocks + 1) * ranks * down_rows
    parcel = pl.pallas_call(
        functools.partial(fetch_kernel, blocks),
        name="fetch",
        out_shape=packet,
        in_specs=[SMEM, VMEM, ANYWHERE, VMEM],
        out_specs=VMEM,
        scratch_shapes=[
            pltpu.VMEM((count, ranks, blocks * features), f32),
            pltpu.SemaphoreType.DMA((count * blocks,)),
        ],
        cost_estimate=cost(0, 4 * packet_bytes),
        compiler_params=LIMIT,
    )(
        id_list,
        id_column,
        down_weight.transpose(0, 2, 1),
        up_weight.transpose(1, 2, 0).reshape(ranks * features, adapters),
    )
    arrived = exchange(parcel)
    core_place = core.astype(jnp.int32).reshape(1)
    down_mine, up_mine, part = pl.pallas_call(
        functools.partial(project_kernel, blocks),
        name="project",
        out_shape=(
            shape((blocks, ranks, shard), bf16),
            shape((blocks, ranks, columns), bf16),
            shape((2 * blocks, ranks, BLOCK), f32),
        ),
        in_specs=[SMEM, VMEM, VMEM, VMEM],
        out_specs=(VMEM, VMEM, VMEM),
        cost_estimate=cost(2 * rows * ranks * (shard + columns), 2 * rows * (shard + total)),
        compiler_params=LIMIT,
    )(core_place, arrived, tok, cot)
    other = core_send(part)
    tiles, low_rank, back_rank = pl.pallas_call(
        functools.partial(tile_kernel, blocks),
        name="tiles",
        out_shape=(packet, shape((rows, ranks), bf16), shape((rows, ranks), bf16)),
        in_specs=[SMEM, VMEM, VMEM, VMEM, VMEM],
        out_specs=(VMEM, VMEM, VMEM),
        cost_estimate=cost(2 * rows * ranks * (shard + columns), 2 * rows * (shard + total)),
        compiler_params=LIMIT,
    )(core_place, part, other, tok, cot)
    owned = exchange(tiles)
    many = adapters // 8
    grad_down, grad_up = pl.pallas_call(
        functools.partial(spread_kernel, blocks),
        name="spread",
        grid=(adapters // many,),
        out_shape=(
            shape((adapters, ranks, down_rows), f32),
            shape((ranks * features, adapters), f32),
        ),
        in_specs=[SMEM, VMEM, VMEM],
        out_specs=(
            pl.BlockSpec((many, ranks, down_rows), lambda i: (i, 0, 0)),
            pl.BlockSpec((ranks * features, adapters), lambda i: (0, 0)),
        ),
        scratch_shapes=[pltpu.VMEM((count, ranks, blocks * features), f32)],
        cost_estimate=cost(0, 4 * adapters * ranks * (down_rows + features)),
        compiler_params=LIMIT,
    )(id_list, id_column, owned)

    kv = out = None
    got_pieces = []
    for c, ((start, depth), own) in enumerate(zip(chunks, held)):
        arrays = [own, mine_y, theirs_y[c]]
        plan = [((0, 0, WHOLE),), ((1, start, MINE), (2, 0, THEIRS))]
        places = [z * 2 + y, z * 2 + 1 - y]
        for step in range(1, layers):
            own = z_send(own)
            layer = (z - step) % layers
            places += [layer * 2 + y, layer * 2 + 1 - y]
            plan += [((len(arrays), 0, WHOLE),), ((len(arrays) + 1, 0, WHOLE),)]
            arrays += [own, y_send(own)]
        last = start + depth == half
        results = chunk_product(
            jnp.stack(places + [x, core]).astype(jnp.int32),
            tuple(plan),
            arrays,
            tok,
            tok_pair,
            cot,
            cot_part,
            cot_rest,
            back_rank,
            down_mine,
            kv,
            out,
            start,
            depth,
            last,
        )
        out, pair = results[:2]
        kv = results[2]
        got_pieces.append(x_send(pair))
    keep, other_columns = results[2:]
    core_got = core_send(other_columns)
    pair_sum = pl.pallas_call(
        kv_pair_kernel,
        name="kv_pair",
        out_shape=shape((rows, columns), bf16),
        in_specs=[VMEM, VMEM],
        out_specs=VMEM,
        cost_estimate=cost(0, 12 * rows * columns),
        compiler_params=LIMIT,
    )(keep, core_got)
    pair_got = x_send(pair_sum)
    key_value = pl.pallas_call(
        kv_kernel,
        name="kv_end",
        out_shape=shape((rows, columns), bf16),
        in_specs=[VMEM] * 5,
        out_specs=VMEM,
        cost_estimate=cost(2 * rows * ranks * columns, 12 * rows * columns),
        compiler_params=LIMIT,
    )(keep, core_got, pair_got, low_rank, up_mine)
    starts = tuple(start for start, _ in chunks)
    out = pl.pallas_call(
        functools.partial(rest_kernel, starts, half),
        name="rest",
        out_shape=shape((rows, shard), bf16),
        in_specs=[SMEM] + [VMEM] * (len(starts) + 1) + [ANYWHERE, ANYWHERE],
        out_specs=ANYWHERE,
        input_output_aliases={len(starts) + 3: 0},
        scratch_shapes=[
            pltpu.VMEM((rows, half), bf16),
            pltpu.VMEM((blocks, ranks, half), bf16),
            pltpu.SemaphoreType.DMA((len(starts) + 1,)),
        ],
        cost_estimate=cost(2 * rows * ranks * half, 4 * rows * half),
        compiler_params=LIMIT,
    )(x.astype(jnp.int32).reshape(1), *got_pieces, back_rank, down_mine, out)
    return (
        key_value.reshape(batches, batch_rows, columns),
        out.reshape(batches, batch_rows, shard),
        grad_down.transpose(0, 2, 1),
        grad_up.reshape(ranks, features, adapters).transpose(2, 0, 1),
    )


def selected_sum(adapter_selector, tiles):
    flat = tiles.reshape(tiles.shape[0], -1)
    return lax.dot_general(
        adapter_selector,
        flat,
        (((0,), (0,)), ((), ())),
        precision=lax.Precision.HIGHEST,
        preferred_element_type=jnp.float32,
    )


def plain(tokens, frozen_weight, cotangent, block_adapter_index, down_weight, up_weight):
    microbatch_list, token_block_rows, shard_width = tokens.shape
    kv_width = cotangent.shape[2]
    key_value_slice = kv_width // lax.axis_size("tp")
    row_total = microbatch_list * token_block_rows
    tok_matrix = tokens.reshape(row_total, shard_width)
    cot_matrix = cotangent.reshape(row_total, kv_width)
    adapter_number = down_weight.shape[0]
    rank_width = down_weight.shape[2]
    adapter_range = jnp.arange(adapter_number, dtype=jnp.int32)
    gathered = lax.all_gather(frozen_weight, "fsdp", axis=1, tiled=True)
    kv_partial = jnp.dot(tok_matrix, gathered, preferred_element_type=jnp.float32)
    frozen_key_value = lax.psum_scatter(kv_partial, "tp", scatter_dimension=1, tiled=True)
    frozen_input_gradient = lax.dot_general(
        cot_matrix, gathered, (((1,), (1,)), ((), ())), preferred_element_type=jnp.float32
    )
    cot_slab = lax.dynamic_slice_in_dim(
        cotangent, lax.axis_index("tp") * key_value_slice, key_value_slice, 2
    )
    fsdp_count = lax.axis_size("fsdp")
    per_dev = token_block_rows // BLOCK
    dest_ids = (
        block_adapter_index.reshape(microbatch_list, fsdp_count, per_dev)
        .transpose(1, 0, 2)
        .reshape(fsdp_count, microbatch_list * per_dev)
    )
    down_send = jnp.take(down_weight, dest_ids, axis=0).transpose(0, 1, 3, 2)
    up_send = jnp.take(up_weight, dest_ids, axis=0)
    down_mine, up_mine = (
        lax.all_to_all(down_send, "fsdp", split_axis=0, concat_axis=3, tiled=True),
        lax.all_to_all(up_send, "fsdp", split_axis=0, concat_axis=3, tiled=True),
    )
    down_mine = down_mine.reshape(microbatch_list, per_dev, rank_width, shard_width)
    up_mine = up_mine.reshape(microbatch_list, per_dev, rank_width, key_value_slice)
    tok_blocks = tokens.reshape(microbatch_list, per_dev, BLOCK, shard_width)
    gradient_blocks = cot_slab.reshape(microbatch_list, per_dev, BLOCK, key_value_slice)
    low_part = jnp.einsum(
        "mnbc,mnrc->mnbr", tok_blocks, down_mine, preferred_element_type=jnp.float32
    )
    partial_input_gradient = adapter_scale * jnp.einsum(
        "fsvj,fsyj->fsvy", gradient_blocks, up_mine, preferred_element_type=jnp.float32
    )
    low_sum, back_sum = lax.psum((low_part, partial_input_gradient), "tp")
    low_rank = low_sum.astype(jnp.bfloat16)
    rank_gradient = back_sum.astype(jnp.bfloat16)
    adapter_key_value = (
        adapter_scale
        * jnp.einsum("elui,elis->elus", low_rank, up_mine, preferred_element_type=jnp.float32)
    ).astype(jnp.bfloat16)
    adapter_input_gradient = jnp.einsum(
        "mnbr,mnrc->mnbc", rank_gradient, down_mine, preferred_element_type=jnp.float32
    ).astype(jnp.bfloat16)
    adapter_key_value = adapter_key_value.reshape(
        microbatch_list, token_block_rows, key_value_slice
    )
    adapter_input_gradient = adapter_input_gradient.reshape(
        microbatch_list, token_block_rows, shard_width
    )
    down_tiles = jnp.einsum(
        "mnbc,mnbr->mnrc", tok_blocks, rank_gradient, preferred_element_type=jnp.float32
    )
    up_weight_tiles = adapter_scale * jnp.einsum(
        "puai,puac->puic", low_rank, gradient_blocks, preferred_element_type=jnp.float32
    )
    down_tiles = down_tiles.reshape(microbatch_list * per_dev, rank_width, shard_width)
    up_weight_tiles = up_weight_tiles.reshape(
        microbatch_list * per_dev, rank_width, key_value_slice
    )
    down_owned, up_owned = (
        lax.all_to_all(
            down_tiles.astype(jnp.bfloat16), "fsdp", split_axis=2, concat_axis=0, tiled=True
        ).astype(down_tiles.dtype),
        lax.all_to_all(
            up_weight_tiles.astype(jnp.bfloat16), "fsdp", split_axis=2, concat_axis=0, tiled=True
        ).astype(up_weight_tiles.dtype),
    )
    owned_ids = dest_ids.reshape(-1)
    adapter_selector = (owned_ids[:, None] == adapter_range[None, :]).astype(jnp.float32)
    grad_down = (
        selected_sum(adapter_selector, down_owned)
        .reshape(adapter_number, rank_width, down_weight.shape[1])
        .transpose(0, 2, 1)
    )
    up_weight_gradient = selected_sum(adapter_selector, up_owned).reshape(up_weight.shape)
    key_value_output = (
        frozen_key_value.reshape(microbatch_list, token_block_rows, key_value_slice)
        + adapter_key_value.astype(jnp.float32)
    ).astype(jnp.bfloat16)
    input_gradient = (
        frozen_input_gradient.reshape(microbatch_list, token_block_rows, shard_width)
        + adapter_input_gradient.astype(jnp.float32)
    ).astype(jnp.bfloat16)
    return (key_value_output, input_gradient, grad_down, up_weight_gradient)


def local(tokens, frozen_weight, cotangent, block_adapter_index, down_weight, up_weight):
    batches, batch_rows, shard = tokens.shape
    blocks = batches * (batch_rows // BLOCK)
    features = up_weight.shape[2]
    fits = (
        lax.axis_size("tp") == 2
        and lax.axis_size("fsdp") % 4 == 0
        and frozen_weight.shape[1] % LANES == 0
        and shard % (16 * 2 * LANES) == 0
        and blocks * features == LANES
        and 2 * features == LANES
        and down_weight.shape[1] > LANES
        and down_weight.shape[0] % (8 * LANES // 2) == 0
    )
    body = paired if fits else plain
    return body(tokens, frozen_weight, cotangent, block_adapter_index, down_weight, up_weight)


def solution(mesh):
    return jax.shard_map(
        local,
        mesh=mesh,
        in_specs=(
            P(None, "fsdp", "tp"),
            P("tp", "fsdp"),
            P(None, "fsdp", None),
            P(),
            P(None, ("tp", "fsdp"), None),
            P(None, None, ("tp", "fsdp")),
        ),
        out_specs=(
            P(None, "fsdp", "tp"),
            P(None, "fsdp", "tp"),
            P(None, ("tp", "fsdp"), None),
            P(None, None, ("tp", "fsdp")),
        ),
        check_vma=False,
    )
```

```python
import functools

import jax
import jax.numpy as jnp
from jax import lax
from jax.experimental import pallas as pl
from jax.experimental.pallas import tpu as pltpu
from jax.sharding import PartitionSpec as P


BLOCK = 128
LANES = 128

adapter_scale = 2.0


ANYWHERE = pl.BlockSpec(memory_space=pl.ANY)
VMEM = pl.BlockSpec(memory_space=pltpu.VMEM)
SMEM = pl.BlockSpec(memory_space=pltpu.SMEM)
LIMIT = pltpu.CompilerParams(vmem_limit_bytes=28 * 1024 * 1024)

ROW_ROW = (((1,), (1,)), ((), ()))


def cost(flops, moved):
    return pl.CostEstimate(flops=flops, bytes_accessed=moved, transcendentals=0)


def dot(left, right, dims=(((1,), (0,)), ((), ()))):
    return lax.dot_general(left, right, dims, preferred_element_type=jnp.float32)


def one_hot(ids, count):
    lane = lax.broadcasted_iota(jnp.int32, (ids.shape[0], count), 1)
    return jnp.where(lane == ids, 1.0, 0.0).astype(jnp.bfloat16)


def send(value, axis, count, route):
    return lax.ppermute(value, axis, [(i, route(i)) for i in range(count)])


def first_kernel(start, half, place, weight, theirs, sem):
    other = pl.multiple_of((1 - place[0]) * half + start, LANES)
    copy = pltpu.make_async_copy(weight.at[pl.ds(other, theirs.shape[0]), :], theirs, sem)
    copy.start()
    copy.wait()


def prep_kernel(start, place, weight, tok, cot, mine, theirs, tok_out, cot_out, sems):
    half = mine.shape[0]
    columns = cot_out.shape[1]
    x, core = place[0], place[1]
    own = pl.multiple_of(x * half, LANES)
    other = pl.multiple_of((1 - x) * half, LANES)
    side = pl.multiple_of(core * columns, LANES)
    copies = [
        pltpu.make_async_copy(
            weight.at[pl.ds(other + start, half - start), :], theirs, sems.at[0]
        ),
        pltpu.make_async_copy(weight.at[pl.ds(own, half), :], mine, sems.at[1]),
        pltpu.make_async_copy(tok.at[:, pl.ds(other, half)], tok_out, sems.at[2]),
        pltpu.make_async_copy(cot.at[:, pl.ds(side, columns)], cot_out, sems.at[3]),
    ]
    for copy in copies:
        copy.start()
    for copy in copies:
        copy.wait()


def pair_kernel(start, place, mine, theirs, out):
    depth, width = theirs.shape
    own = pl.ds(pl.multiple_of(place[0] * width, LANES), width)
    other = pl.ds(pl.multiple_of((1 - place[0]) * width, LANES), width)
    out[:, own] = mine[pl.ds(start, depth), :]
    out[:, other] = theirs[...]


WHOLE, MINE, THEIRS = 0, 1, 2


def chunk_kernel(plan, array_count, has_kv, last, start, half, *refs):
    refs = list(refs)
    take = lambda n: [refs.pop(0) for _ in range(n)]
    (place,) = take(1)
    arrays = take(array_count)
    tok_all, tok_pair, cot_own, cot_part, cot_rest = take(5)
    (kv_in,) = take(1) if has_kv else (None,)
    ig_own, ig_pair = take(2)
    kv_out = take(2) if last else take(1)
    weight, tok, cot = refs[:3]
    rows = tok_all.shape[0]
    depth, total = weight.shape
    count = len(plan)
    width = total // count
    columns = cot_part.shape[1]
    x, core = place[count], place[count + 1]
    base = pl.multiple_of(x * half + start, LANES)
    lower = pl.ds(rows, rows)
    tok[pl.ds(0, rows), :] = tok_all[:, pl.ds(base, depth)]
    tok[lower, :] = tok_pair[:, pl.ds(start, depth)]
    for i, pieces in enumerate(plan):
        for array, offset, kind in pieces:
            wide = arrays[array].shape[1]
            shift = {WHOLE: 0, MINE: x * wide, THEIRS: (1 - x) * wide}[kind]
            target = pl.ds(pl.multiple_of(place[i] * width + shift, LANES), wide)
            weight[:, target] = arrays[array][pl.ds(offset, depth), :]
        at = pl.ds(pl.multiple_of(place[i] * width, LANES), width)
        part = dot(tok[...], weight[:, at])
        if has_kv:
            part = part + kv_in[:, at]
        if last:
            wide_kv, narrow_kv = refs[3:]
            slot = pl.ds(pl.multiple_of(lax.rem(place[i] * width, columns), LANES), width)
            where = lax.rem(lax.div(place[i] * width, columns) + core, 2)
            wide_kv[where, :, slot] = part
            narrow_kv[where, :, slot] = part.astype(narrow_kv.dtype)
        else:
            kv_out[0][:, at] = part
    if last:
        kv_out[0][...] = wide_kv[0]
        kv_out[1][...] = narrow_kv[1]
    cot[pl.ds(0, rows), :] = cot_own[...]
    cot[lower, pl.ds(pl.multiple_of(core * columns, LANES), columns)] = cot_part[...]
    cot[lower, pl.ds(pl.multiple_of((1 - core) * columns, LANES), columns)] = cot_rest[...]
    tile = min(2 * LANES, depth)

    @pl.loop(0, depth // tile)
    def _(step):
        at = pl.multiple_of(step * tile, tile)
        part = dot(cot[...], weight[pl.ds(at, tile), :], ROW_ROW)
        ig_own[:, pl.ds(at, tile)] = part[:rows]
        ig_pair[:, pl.ds(at, tile)] = part[rows:].astype(ig_pair.dtype)


def chunk_product(
    place, plan, arrays, tok, tok_pair, cot, cot_part, cot_rest, kv, start, depth, last
):
    rows, half = tok_pair.shape
    total = cot.shape[1]
    operands = [place, *arrays, tok, tok_pair, cot, cot_part, cot_rest]
    if kv is not None:
        operands.append(kv)
    shape = jax.ShapeDtypeStruct
    shapes = [shape((rows, depth), jnp.float32), shape((rows, depth), jnp.bfloat16)]
    if last:
        shapes.append(shape((2 * rows, total // 2), jnp.float32))
        shapes.append(shape((2 * rows, total // 2), jnp.bfloat16))
    else:
        shapes.append(shape((2 * rows, total), jnp.float32))
    return pl.pallas_call(
        functools.partial(chunk_kernel, plan, len(arrays), kv is not None, last, start, half),
        out_shape=tuple(shapes),
        in_specs=[SMEM] + [VMEM] * (len(operands) - 1),
        out_specs=(VMEM,) * len(shapes),
        scratch_shapes=[
            pltpu.VMEM((depth, total), jnp.bfloat16),
            pltpu.VMEM((2 * rows, depth), jnp.bfloat16),
            pltpu.VMEM((2 * rows, total), jnp.bfloat16),
        ]
        + [pltpu.VMEM((2, 2 * rows, total // 2), kind) for kind in (jnp.float32, jnp.bfloat16) if last],
        cost_estimate=cost(8 * rows * depth * total, 2 * depth * total + 16 * rows * total),
        compiler_params=LIMIT,
    )(*operands)


def fetch_kernel(blocks, ids, ids_column, down, up, out, scratch, sems):
    devices, ranks = out.shape[0], down.shape[1]
    features = up.shape[0] // ranks
    copies = []
    for i in range(devices * blocks):
        copies.append(
            pltpu.make_async_copy(
                down.at[ids[i]],
                out.at[i // blocks, pl.ds(i % blocks * ranks, ranks), :],
                sems.at[i],
            )
        )
        copies[-1].start()
    count = up.shape[1]
    chosen = [one_hot(ids_column[pl.ds(m * devices, devices), :], count) for m in range(blocks)]
    for r in range(ranks):
        rows = up[pl.ds(r * features, features), :]
        scratch[:, r, :] = jnp.concatenate([dot(c, rows, ROW_ROW) for c in chosen], axis=1)
    lanes = blocks * features
    packed = scratch[...].astype(out.dtype)
    out[:, pl.ds(blocks * ranks, ranks), pl.ds(0, lanes)] = packed
    rest = out.shape[2] - lanes
    out[:, pl.ds(blocks * ranks, ranks), pl.ds(lanes, rest)] = jnp.zeros(
        (devices, ranks, rest), out.dtype
    )
    for copy in copies:
        copy.wait()


def project_kernel(blocks, core_ref, got, tok, cot, down_out, up_out, part):
    devices, ranks = got.shape[0], part.shape[1]
    width = got.shape[2]
    columns = up_out.shape[2]
    features = columns // devices
    at = pl.ds(pl.multiple_of(core_ref[0] * columns, LANES), columns)
    for m in range(blocks):
        for d in range(devices):
            down_out[m, :, pl.ds(d * width, width)] = got[d, pl.ds(m * ranks, ranks), :]
        lane = pl.ds(m * features, features)
        row = pl.ds(blocks * ranks, ranks)
        for d in range(0, devices, 2):
            up_out[m, :, pl.ds(d * features, 2 * features)] = jnp.concatenate(
                [got[d, row, lane], got[d + 1, row, lane]], axis=1
            )
        own = pl.ds(m * BLOCK, BLOCK)
        part[m] = dot(down_out[m], tok[own, :], ROW_ROW)
        part[blocks + m] = adapter_scale * dot(up_out[m], cot[own, at], ROW_ROW)


def tile_kernel(blocks, core_ref, part, other, tok, cot, out, low_out, back_out):
    devices, ranks, width = out.shape[0], part.shape[1], out.shape[2]
    columns = cot.shape[1] // 2
    features = columns // devices
    at = pl.ds(pl.multiple_of(core_ref[0] * columns, LANES), columns)
    summed = part[...] + other[...]
    ups = []
    for m in range(blocks):
        own = pl.ds(m * BLOCK, BLOCK)
        low = summed[m].astype(jnp.bfloat16)
        back = summed[blocks + m].astype(jnp.bfloat16)
        low_out[own, :] = jnp.transpose(summed[m]).astype(jnp.bfloat16)
        back_out[own, :] = jnp.transpose(summed[blocks + m]).astype(jnp.bfloat16)
        for d in range(devices):
            piece = dot(back, tok[own, pl.ds(d * width, width)])
            out[d, pl.ds(m * ranks, ranks), :] = piece.astype(out.dtype)
        ups.append(adapter_scale * dot(low, cot[own, at]))
    lanes = blocks * features
    for d in range(devices):
        piece = jnp.concatenate([u[:, d * features : (d + 1) * features] for u in ups], axis=1)
        out[d, pl.ds(blocks * ranks, ranks), pl.ds(0, lanes)] = piece.astype(out.dtype)
    rest = width - lanes
    out[:, pl.ds(blocks * ranks, ranks), pl.ds(lanes, rest)] = jnp.zeros(
        (devices, ranks, rest), out.dtype
    )


def spread_kernel(blocks, ids, ids_column, got, down_out, up_out, scratch):
    step = pl.program_id(0)
    many, ranks = down_out.shape[0], down_out.shape[1]
    devices = got.shape[0]
    down_out[...] = jnp.zeros(down_out.shape, down_out.dtype)
    for i in range(devices * blocks):
        where = ids[i] - step * many

        @pl.when((where >= 0) & (where < many))
        def _():
            tile = got[i // blocks, pl.ds(i % blocks * ranks, ranks), :].astype(jnp.float32)
            down_out[where] = down_out[where] + tile

    @pl.when(step == 0)
    def _():
        count = up_out.shape[1]
        features = up_out.shape[0] // ranks
        scratch[...] = got[:, pl.ds(blocks * ranks, ranks), pl.ds(0, blocks * features)].astype(
            jnp.float32
        )
        chosen = [one_hot(ids_column[pl.ds(m * devices, devices), :], count) for m in range(blocks)]
        for r in range(ranks):
            turned = jnp.transpose(scratch[:, r, :]).astype(jnp.bfloat16)
            total = 0.0
            for m in range(blocks):
                total = total + dot(turned[m * features : (m + 1) * features], chosen[m])
            up_out[pl.ds(r * features, features), :] = total


def kv_pair_kernel(keep, got, out):
    rows = out.shape[0]
    lower = pl.ds(rows, rows)
    out[...] = (keep[lower, :] + got[lower, :].astype(jnp.float32)).astype(out.dtype)


def kv_kernel(keep, core_got, pair_got, low, up, out):
    rows = out.shape[0]
    for m in range(rows // BLOCK):
        own = pl.ds(m * BLOCK, BLOCK)
        base = keep[own, :] + core_got[own, :].astype(jnp.float32)
        base = base + pair_got[own, :].astype(jnp.float32)
        adapter = adapter_scale * dot(low[own, :], up[m])
        adapter = adapter.astype(jnp.bfloat16).astype(jnp.float32)
        out[own, :] = (base + adapter).astype(out.dtype)


def finish_kernel(starts, half, own, place, *refs):
    count = len(starts)
    sums, (back, down), refs = refs[:count], refs[count : count + 2], refs[count + 2 :]
    out, finished, sems = refs[-3:]
    x = place[0] if own else 1 - place[0]
    base = pl.multiple_of(x * half, LANES)
    copies = []
    for i, start in enumerate(starts):
        depth = sums[i].shape[1]
        at = pl.ds(pl.multiple_of(base + start, LANES), depth)
        for m in range(down.shape[0]):
            rows = pl.ds(m * BLOCK, BLOCK)
            adapter = dot(back[rows, :], down[m, :, at]).astype(jnp.bfloat16)
            both = sums[i][rows, :].astype(jnp.float32) + adapter.astype(jnp.float32)
            finished[rows, pl.ds(start, depth)] = both.astype(finished.dtype)
        copies.append(
            pltpu.make_async_copy(finished.at[:, pl.ds(start, depth)], out.at[:, at], sems.at[i])
        )
        copies[-1].start()
    for copy in copies:
        copy.wait()


def finish(starts, place, sums, back, down, out):
    rows = sums[0].shape[0]
    half = sum(piece.shape[1] for piece in sums)
    ranks = down.shape[1]
    operands = [place, *sums, back, down]
    specs = [SMEM] + [VMEM] * (len(operands) - 1)
    aliases = {}
    if out is not None:
        aliases[len(operands)] = 0
        operands.append(out)
        specs.append(ANYWHERE)
    return pl.pallas_call(
        functools.partial(finish_kernel, starts, half, out is None),
        out_shape=jax.ShapeDtypeStruct((rows, 2 * half), jnp.bfloat16),
        in_specs=specs,
        out_specs=ANYWHERE,
        input_output_aliases=aliases,
        scratch_shapes=[
            pltpu.VMEM((rows, half), jnp.bfloat16),
            pltpu.SemaphoreType.DMA((len(starts),)),
        ],
        cost_estimate=cost(2 * rows * ranks * half, 8 * rows * half),
        compiler_params=LIMIT,
    )(*operands)


def paired(tokens, frozen_weight, cotangent, block_adapter_index, down_weight, up_weight):
    batches, batch_rows, shard = tokens.shape
    total = cotangent.shape[2]
    columns = total // 2
    rows = batches * batch_rows
    half = shard // 2
    tok = tokens.reshape(rows, shard)
    cot = cotangent.reshape(rows, total)
    adapters, down_rows, ranks = down_weight.shape
    features = up_weight.shape[2]
    per_device = batch_rows // BLOCK
    blocks = batches * per_device
    count = lax.axis_size("fsdp")
    layers = count // 4
    index = lax.axis_index("fsdp")
    core = lax.axis_index("tp")
    x, y, z = index % 2, (index // 2) % 2, index // 4
    bf16, f32 = jnp.bfloat16, jnp.float32
    shape = jax.ShapeDtypeStruct

    def move(axis, width, route, value):
        return send(value, axis, width, route)

    x_send = lambda v: move("fsdp", count, lambda i: i ^ 1, v)
    y_send = lambda v: move("fsdp", count, lambda i: i ^ 2, v)
    z_send = lambda v: move("fsdp", count, lambda i: (i + 4) % count, v)
    core_send = lambda v: move("tp", 2, lambda i: i ^ 1, v)

    chunks = ((0, half // 2), (half // 2, half // 2))
    block = frozen_weight.shape[1]
    here = jnp.stack([x, core]).astype(jnp.int32)
    split = chunks[1][0]
    theirs = [
        pl.pallas_call(
            functools.partial(first_kernel, 0, half),
            name="first",
            out_shape=shape((split, block), bf16),
            in_specs=[SMEM, ANYWHERE],
            out_specs=VMEM,
            scratch_shapes=[pltpu.SemaphoreType.DMA],
            cost_estimate=cost(0, 4 * split * block),
            compiler_params=LIMIT,
        )(here, frozen_weight)
    ]
    mine, later, tok_sent, cot_sent = pl.pallas_call(
        functools.partial(prep_kernel, split),
        name="prep",
        out_shape=(
            shape((half, block), bf16),
            shape((half - split, block), bf16),
            shape((rows, half), bf16),
            shape((rows, columns), bf16),
        ),
        in_specs=[SMEM, ANYWHERE, ANYWHERE, ANYWHERE],
        out_specs=(VMEM,) * 4,
        scratch_shapes=[pltpu.SemaphoreType.DMA((4,))],
        cost_estimate=cost(0, 4 * (2 * half * block + rows * (half + columns))),
        compiler_params=LIMIT,
    )(here, frozen_weight, tok, cot)
    theirs.append(later)
    mine_y = y_send(mine)
    tok_pair = x_send(tok_sent)
    cot_part = x_send(cot_sent)
    cot_rest = core_send(cot_part)
    held, theirs_y = [], []
    for c, (start, depth) in enumerate(chunks):
        got = x_send(theirs[c])
        held.append(
            pl.pallas_call(
                functools.partial(pair_kernel, start),
                out_shape=shape((depth, 2 * block), bf16),
                in_specs=[SMEM, VMEM, VMEM],
                out_specs=VMEM,
                cost_estimate=cost(0, 8 * depth * block),
                compiler_params=LIMIT,
            )(here, mine, got)
        )
        theirs_y.append(y_send(got))

    ids = (
        block_adapter_index.reshape(batches, count, per_device)
        .transpose(1, 0, 2)
        .reshape(count, blocks)
    )
    id_list = ids.reshape(-1)
    id_column = ids.T.reshape(-1, 1)

    def exchange(value):
        return lax.all_to_all(value, "fsdp", split_axis=0, concat_axis=0, tiled=True)

    packet = shape((count, (blocks + 1) * ranks, down_rows), bf16)
    packet_bytes = 2 * count * (blocks + 1) * ranks * down_rows
    parcel = pl.pallas_call(
        functools.partial(fetch_kernel, blocks),
        name="fetch",
        out_shape=packet,
        in_specs=[SMEM, VMEM, ANYWHERE, VMEM],
        out_specs=VMEM,
        scratch_shapes=[
            pltpu.VMEM((count, ranks, blocks * features), f32),
            pltpu.SemaphoreType.DMA((count * blocks,)),
        ],
        cost_estimate=cost(0, 4 * packet_bytes),
        compiler_params=LIMIT,
    )(
        id_list,
        id_column,
        down_weight.transpose(0, 2, 1),
        up_weight.transpose(1, 2, 0).reshape(ranks * features, adapters),
    )
    arrived = exchange(parcel)
    core_place = core.astype(jnp.int32).reshape(1)
    down_mine, up_mine, part = pl.pallas_call(
        functools.partial(project_kernel, blocks),
        name="project",
        out_shape=(
            shape((blocks, ranks, shard), bf16),
            shape((blocks, ranks, columns), bf16),
            shape((2 * blocks, ranks, BLOCK), f32),
        ),
        in_specs=[SMEM, VMEM, VMEM, VMEM],
        out_specs=(VMEM, VMEM, VMEM),
        cost_estimate=cost(2 * rows * ranks * (shard + columns), 2 * rows * (shard + total)),
        compiler_params=LIMIT,
    )(core_place, arrived, tok, cot)
    other = core_send(part)
    tiles, low_rank, back_rank = pl.pallas_call(
        functools.partial(tile_kernel, blocks),
        name="tiles",
        out_shape=(packet, shape((rows, ranks), bf16), shape((rows, ranks), bf16)),
        in_specs=[SMEM, VMEM, VMEM, VMEM, VMEM],
        out_specs=(VMEM, VMEM, VMEM),
        cost_estimate=cost(2 * rows * ranks * (shard + columns), 2 * rows * (shard + total)),
        compiler_params=LIMIT,
    )(core_place, part, other, tok, cot)
    owned = exchange(tiles)
    many = adapters // 8
    grad_down, grad_up = pl.pallas_call(
        functools.partial(spread_kernel, blocks),
        name="spread",
        grid=(adapters // many,),
        out_shape=(
            shape((adapters, ranks, down_rows), f32),
            shape((ranks * features, adapters), f32),
        ),
        in_specs=[SMEM, VMEM, VMEM],
        out_specs=(
            pl.BlockSpec((many, ranks, down_rows), lambda i: (i, 0, 0)),
            pl.BlockSpec((ranks * features, adapters), lambda i: (0, 0)),
        ),
        scratch_shapes=[pltpu.VMEM((count, ranks, blocks * features), f32)],
        cost_estimate=cost(0, 4 * adapters * ranks * (down_rows + features)),
        compiler_params=LIMIT,
    )(id_list, id_column, owned)

    kv = None
    got_pieces, own_pieces = [], []
    for c, ((start, depth), own) in enumerate(zip(chunks, held)):
        arrays = [own, mine_y, theirs_y[c]]
        plan = [((0, 0, WHOLE),), ((1, start, MINE), (2, 0, THEIRS))]
        places = [z * 2 + y, z * 2 + 1 - y]
        for step in range(1, layers):
            own = z_send(own)
            layer = (z - step) % layers
            places += [layer * 2 + y, layer * 2 + 1 - y]
            plan += [((len(arrays), 0, WHOLE),), ((len(arrays) + 1, 0, WHOLE),)]
            arrays += [own, y_send(own)]
        last = start + depth == half
        results = chunk_product(
            jnp.stack(places + [x, core]).astype(jnp.int32),
            tuple(plan),
            arrays,
            tok,
            tok_pair,
            cot,
            cot_part,
            cot_rest,
            kv,
            start,
            depth,
            last,
        )
        own_sum, pair = results[:2]
        own_pieces.append(own_sum)
        kv = results[2]
        got_pieces.append(x_send(pair))
    keep, other_columns = results[2:]
    core_got = core_send(other_columns)
    pair_sum = pl.pallas_call(
        kv_pair_kernel,
        name="kv_pair",
        out_shape=shape((rows, columns), bf16),
        in_specs=[VMEM, VMEM],
        out_specs=VMEM,
        cost_estimate=cost(0, 12 * rows * columns),
        compiler_params=LIMIT,
    )(keep, core_got)
    pair_got = x_send(pair_sum)
    key_value = pl.pallas_call(
        kv_kernel,
        name="kv_end",
        out_shape=shape((rows, columns), bf16),
        in_specs=[VMEM] * 5,
        out_specs=VMEM,
        cost_estimate=cost(2 * rows * ranks * columns, 12 * rows * columns),
        compiler_params=LIMIT,
    )(keep, core_got, pair_got, low_rank, up_mine)
    starts = tuple(start for start, _ in chunks)
    out = finish(starts, here, own_pieces, back_rank, down_mine, None)
    out = finish(starts, here, got_pieces, back_rank, down_mine, out)
    return (
        key_value.reshape(batches, batch_rows, columns),
        out.reshape(batches, batch_rows, shard),
        grad_down.transpose(0, 2, 1),
        grad_up.reshape(ranks, features, adapters).transpose(2, 0, 1),
    )


def selected_sum(adapter_selector, tiles):
    flat = tiles.reshape(tiles.shape[0], -1)
    return lax.dot_general(
        adapter_selector,
        flat,
        (((0,), (0,)), ((), ())),
        precision=lax.Precision.HIGHEST,
        preferred_element_type=jnp.float32,
    )


def plain(tokens, frozen_weight, cotangent, block_adapter_index, down_weight, up_weight):
    microbatch_list, token_block_rows, shard_width = tokens.shape
    kv_width = cotangent.shape[2]
    key_value_slice = kv_width // lax.axis_size("tp")
    row_total = microbatch_list * token_block_rows
    tok_matrix = tokens.reshape(row_total, shard_width)
    cot_matrix = cotangent.reshape(row_total, kv_width)
    adapter_number = down_weight.shape[0]
    rank_width = down_weight.shape[2]
    adapter_range = jnp.arange(adapter_number, dtype=jnp.int32)
    gathered = lax.all_gather(frozen_weight, "fsdp", axis=1, tiled=True)
    kv_partial = jnp.dot(tok_matrix, gathered, preferred_element_type=jnp.float32)
    frozen_key_value = lax.psum_scatter(kv_partial, "tp", scatter_dimension=1, tiled=True)
    frozen_input_gradient = lax.dot_general(
        cot_matrix, gathered, (((1,), (1,)), ((), ())), preferred_element_type=jnp.float32
    )
    cot_slab = lax.dynamic_slice_in_dim(
        cotangent, lax.axis_index("tp") * key_value_slice, key_value_slice, 2
    )
    fsdp_count = lax.axis_size("fsdp")
    per_dev = token_block_rows // BLOCK
    dest_ids = (
        block_adapter_index.reshape(microbatch_list, fsdp_count, per_dev)
        .transpose(1, 0, 2)
        .reshape(fsdp_count, microbatch_list * per_dev)
    )
    down_send = jnp.take(down_weight, dest_ids, axis=0).transpose(0, 1, 3, 2)
    up_send = jnp.take(up_weight, dest_ids, axis=0)
    down_mine, up_mine = (
        lax.all_to_all(down_send, "fsdp", split_axis=0, concat_axis=3, tiled=True),
        lax.all_to_all(up_send, "fsdp", split_axis=0, concat_axis=3, tiled=True),
    )
    down_mine = down_mine.reshape(microbatch_list, per_dev, rank_width, shard_width)
    up_mine = up_mine.reshape(microbatch_list, per_dev, rank_width, key_value_slice)
    tok_blocks = tokens.reshape(microbatch_list, per_dev, BLOCK, shard_width)
    gradient_blocks = cot_slab.reshape(microbatch_list, per_dev, BLOCK, key_value_slice)
    low_part = jnp.einsum(
        "mnbc,mnrc->mnbr", tok_blocks, down_mine, preferred_element_type=jnp.float32
    )
    partial_input_gradient = adapter_scale * jnp.einsum(
        "fsvj,fsyj->fsvy", gradient_blocks, up_mine, preferred_element_type=jnp.float32
    )
    low_sum, back_sum = lax.psum((low_part, partial_input_gradient), "tp")
    low_rank = low_sum.astype(jnp.bfloat16)
    rank_gradient = back_sum.astype(jnp.bfloat16)
    adapter_key_value = (
        adapter_scale
        * jnp.einsum("elui,elis->elus", low_rank, up_mine, preferred_element_type=jnp.float32)
    ).astype(jnp.bfloat16)
    adapter_input_gradient = jnp.einsum(
        "mnbr,mnrc->mnbc", rank_gradient, down_mine, preferred_element_type=jnp.float32
    ).astype(jnp.bfloat16)
    adapter_key_value = adapter_key_value.reshape(
        microbatch_list, token_block_rows, key_value_slice
    )
    adapter_input_gradient = adapter_input_gradient.reshape(
        microbatch_list, token_block_rows, shard_width
    )
    down_tiles = jnp.einsum(
        "mnbc,mnbr->mnrc", tok_blocks, rank_gradient, preferred_element_type=jnp.float32
    )
    up_weight_tiles = adapter_scale * jnp.einsum(
        "puai,puac->puic", low_rank, gradient_blocks, preferred_element_type=jnp.float32
    )
    down_tiles = down_tiles.reshape(microbatch_list * per_dev, rank_width, shard_width)
    up_weight_tiles = up_weight_tiles.reshape(
        microbatch_list * per_dev, rank_width, key_value_slice
    )
    down_owned, up_owned = (
        lax.all_to_all(
            down_tiles.astype(jnp.bfloat16), "fsdp", split_axis=2, concat_axis=0, tiled=True
        ).astype(down_tiles.dtype),
        lax.all_to_all(
            up_weight_tiles.astype(jnp.bfloat16), "fsdp", split_axis=2, concat_axis=0, tiled=True
        ).astype(up_weight_tiles.dtype),
    )
    owned_ids = dest_ids.reshape(-1)
    adapter_selector = (owned_ids[:, None] == adapter_range[None, :]).astype(jnp.float32)
    grad_down = (
        selected_sum(adapter_selector, down_owned)
        .reshape(adapter_number, rank_width, down_weight.shape[1])
        .transpose(0, 2, 1)
    )
    up_weight_gradient = selected_sum(adapter_selector, up_owned).reshape(up_weight.shape)
    key_value_output = (
        frozen_key_value.reshape(microbatch_list, token_block_rows, key_value_slice)
        + adapter_key_value.astype(jnp.float32)
    ).astype(jnp.bfloat16)
    input_gradient = (
        frozen_input_gradient.reshape(microbatch_list, token_block_rows, shard_width)
        + adapter_input_gradient.astype(jnp.float32)
    ).astype(jnp.bfloat16)
    return (key_value_output, input_gradient, grad_down, up_weight_gradient)


def local(tokens, frozen_weight, cotangent, block_adapter_index, down_weight, up_weight):
    batches, batch_rows, shard = tokens.shape
    blocks = batches * (batch_rows // BLOCK)
    features = up_weight.shape[2]
    fits = (
        lax.axis_size("tp") == 2
        and lax.axis_size("fsdp") % 4 == 0
        and frozen_weight.shape[1] % LANES == 0
        and shard % (16 * 2 * LANES) == 0
        and blocks * features == LANES
        and 2 * features == LANES
        and down_weight.shape[1] > LANES
        and down_weight.shape[0] % (8 * LANES // 2) == 0
    )
    body = paired if fits else plain
    return body(tokens, frozen_weight, cotangent, block_adapter_index, down_weight, up_weight)


def solution(mesh):
    return jax.shard_map(
        local,
        mesh=mesh,
        in_specs=(
            P(None, "fsdp", "tp"),
            P("tp", "fsdp"),
            P(None, "fsdp", None),
            P(),
            P(None, ("tp", "fsdp"), None),
            P(None, None, ("tp", "fsdp")),
        ),
        out_specs=(
            P(None, "fsdp", "tp"),
            P(None, "fsdp", "tp"),
            P(None, ("tp", "fsdp"), None),
            P(None, None, ("tp", "fsdp")),
        ),
        check_vma=False,
    )
```

```python
import functools

import jax
import jax.numpy as jnp
from jax import lax
from jax.experimental import pallas as pl
from jax.experimental.pallas import tpu as pltpu
from jax.sharding import PartitionSpec as P


BLOCK = 128
LANES = 128

adapter_scale = 2.0


ANYWHERE = pl.BlockSpec(memory_space=pl.ANY)
VMEM = pl.BlockSpec(memory_space=pltpu.VMEM)
SMEM = pl.BlockSpec(memory_space=pltpu.SMEM)
LIMIT = pltpu.CompilerParams(vmem_limit_bytes=28 * 1024 * 1024)

ROW_ROW = (((1,), (1,)), ((), ()))


def cost(flops, moved):
    return pl.CostEstimate(flops=flops, bytes_accessed=moved, transcendentals=0)


def dot(left, right, dims=(((1,), (0,)), ((), ()))):
    return lax.dot_general(left, right, dims, preferred_element_type=jnp.float32)


def one_hot(ids, count):
    lane = lax.broadcasted_iota(jnp.int32, (ids.shape[0], count), 1)
    return jnp.where(lane == ids, 1.0, 0.0).astype(jnp.bfloat16)


def send(value, axis, count, route):
    return lax.ppermute(value, axis, [(i, route(i)) for i in range(count)])


def first_kernel(start, half, place, weight, theirs, sem):
    other = pl.multiple_of((1 - place[0]) * half + start, LANES)
    copy = pltpu.make_async_copy(weight.at[pl.ds(other, theirs.shape[0]), :], theirs, sem)
    copy.start()
    copy.wait()


def prep_kernel(start, place, weight, tok, cot, mine, theirs, tok_out, cot_out, sems):
    half = mine.shape[0]
    columns = cot_out.shape[1]
    x, core = place[0], place[1]
    own = pl.multiple_of(x * half, LANES)
    other = pl.multiple_of((1 - x) * half, LANES)
    side = pl.multiple_of(core * columns, LANES)
    copies = [
        pltpu.make_async_copy(
            weight.at[pl.ds(other + start, half - start), :], theirs, sems.at[0]
        ),
        pltpu.make_async_copy(weight.at[pl.ds(own, half), :], mine, sems.at[1]),
        pltpu.make_async_copy(tok.at[:, pl.ds(other, half)], tok_out, sems.at[2]),
        pltpu.make_async_copy(cot.at[:, pl.ds(side, columns)], cot_out, sems.at[3]),
    ]
    for copy in copies:
        copy.start()
    for copy in copies:
        copy.wait()


def pair_kernel(start, place, mine, theirs, out):
    depth, width = theirs.shape
    own = pl.ds(pl.multiple_of(place[0] * width, LANES), width)
    other = pl.ds(pl.multiple_of((1 - place[0]) * width, LANES), width)
    out[:, own] = mine[pl.ds(start, depth), :]
    out[:, other] = theirs[...]


WHOLE, MINE, THEIRS = 0, 1, 2


def chunk_kernel(plan, array_count, modes, has_kv, last, start, half, *refs):
    refs = list(refs)
    take = lambda n: [refs.pop(0) for _ in range(n)]
    (place,) = take(1)
    arrays = take(array_count)
    tok_all, tok_pair, cot_own, cot_part, cot_rest = take(5)
    (kv_in,) = take(1) if has_kv else (None,)
    forward, backward = "kv" in modes, "ig" in modes
    ig_own, ig_pair = take(2) if backward else (None, None)
    kv_out = take(1 + last) if forward else None
    weight, tok, cot = refs[:3]
    rows = tok_all.shape[0]
    depth, total = weight.shape
    count = len(plan)
    width = total // count
    columns = cot_part.shape[1]
    x, core = place[count], place[count + 1]
    base = pl.multiple_of(x * half + start, LANES)
    lower = pl.ds(rows, rows)
    if forward:
        tok[pl.ds(0, rows), :] = tok_all[:, pl.ds(base, depth)]
        tok[lower, :] = tok_pair[:, pl.ds(start, depth)]
    for i, pieces in enumerate(plan):
        for array, offset, kind in pieces:
            wide = arrays[array].shape[1]
            shift = {WHOLE: 0, MINE: x * wide, THEIRS: (1 - x) * wide}[kind]
            target = pl.ds(pl.multiple_of(place[i] * width + shift, LANES), wide)
            weight[:, target] = arrays[array][pl.ds(offset, depth), :]
        at = pl.ds(pl.multiple_of(place[i] * width, LANES), width)
        if not forward:
            continue
        part = dot(tok[...], weight[:, at])
        if has_kv:
            part = part + kv_in[:, at]
        if last:
            wide_kv, narrow_kv = refs[3:]
            slot = pl.ds(pl.multiple_of(lax.rem(place[i] * width, columns), LANES), width)
            where = lax.rem(lax.div(place[i] * width, columns) + core, 2)
            wide_kv[where, :, slot] = part
            narrow_kv[where, :, slot] = part.astype(narrow_kv.dtype)
        else:
            kv_out[0][:, at] = part
    if last and forward:
        kv_out[0][...] = wide_kv[0]
        kv_out[1][...] = narrow_kv[1]
    if not backward:
        return
    cot[pl.ds(0, rows), :] = cot_own[...]
    cot[lower, pl.ds(pl.multiple_of(core * columns, LANES), columns)] = cot_part[...]
    cot[lower, pl.ds(pl.multiple_of((1 - core) * columns, LANES), columns)] = cot_rest[...]
    tile = min(2 * LANES, depth)

    @pl.loop(0, depth // tile)
    def _(step):
        at = pl.multiple_of(step * tile, tile)
        part = dot(cot[...], weight[pl.ds(at, tile), :], ROW_ROW)
        ig_own[:, pl.ds(at, tile)] = part[:rows]
        ig_pair[:, pl.ds(at, tile)] = part[rows:].astype(ig_pair.dtype)


def chunk_product(
    place, plan, arrays, tok, tok_pair, cot, cot_part, cot_rest, kv, start, depth, last, modes
):
    rows, half = tok_pair.shape
    total = cot.shape[1]
    operands = [place, *arrays, tok, tok_pair, cot, cot_part, cot_rest]
    if kv is not None:
        operands.append(kv)
    shape = jax.ShapeDtypeStruct
    shapes = []
    if "ig" in modes:
        shapes += [shape((rows, depth), jnp.float32), shape((rows, depth), jnp.bfloat16)]
    if "kv" not in modes:
        pass
    elif last:
        shapes.append(shape((2 * rows, total // 2), jnp.float32))
        shapes.append(shape((2 * rows, total // 2), jnp.bfloat16))
    else:
        shapes.append(shape((2 * rows, total), jnp.float32))
    return pl.pallas_call(
        functools.partial(chunk_kernel, plan, len(arrays), modes, kv is not None, last, start, half),
        out_shape=tuple(shapes),
        in_specs=[SMEM] + [VMEM] * (len(operands) - 1),
        out_specs=(VMEM,) * len(shapes),
        scratch_shapes=[
            pltpu.VMEM((depth, total), jnp.bfloat16),
            pltpu.VMEM((2 * rows, depth), jnp.bfloat16),
            pltpu.VMEM((2 * rows, total), jnp.bfloat16),
        ]
        + [pltpu.VMEM((2, 2 * rows, total // 2), kind) for kind in (jnp.float32, jnp.bfloat16) if last and "kv" in modes],
        cost_estimate=cost(4 * len(modes) * rows * depth * total, 2 * depth * total + 16 * rows * total),
        compiler_params=LIMIT,
    )(*operands)


def fetch_kernel(blocks, ids, ids_column, down, up, out, scratch, sems):
    devices, ranks = out.shape[0], down.shape[1]
    features = up.shape[0] // ranks
    copies = []
    for i in range(devices * blocks):
        copies.append(
            pltpu.make_async_copy(
                down.at[ids[i]],
                out.at[i // blocks, pl.ds(i % blocks * ranks, ranks), :],
                sems.at[i],
            )
        )
        copies[-1].start()
    count = up.shape[1]
    chosen = [one_hot(ids_column[pl.ds(m * devices, devices), :], count) for m in range(blocks)]
    for r in range(ranks):
        rows = up[pl.ds(r * features, features), :]
        scratch[:, r, :] = jnp.concatenate([dot(c, rows, ROW_ROW) for c in chosen], axis=1)
    lanes = blocks * features
    packed = scratch[...].astype(out.dtype)
    out[:, pl.ds(blocks * ranks, ranks), pl.ds(0, lanes)] = packed
    rest = out.shape[2] - lanes
    out[:, pl.ds(blocks * ranks, ranks), pl.ds(lanes, rest)] = jnp.zeros(
        (devices, ranks, rest), out.dtype
    )
    for copy in copies:
        copy.wait()


def project_kernel(blocks, core_ref, got, tok, cot, down_out, up_out, part):
    devices, ranks = got.shape[0], part.shape[1]
    width = got.shape[2]
    columns = up_out.shape[2]
    features = columns // devices
    at = pl.ds(pl.multiple_of(core_ref[0] * columns, LANES), columns)
    for m in range(blocks):
        for d in range(devices):
            down_out[m, :, pl.ds(d * width, width)] = got[d, pl.ds(m * ranks, ranks), :]
        lane = pl.ds(m * features, features)
        row = pl.ds(blocks * ranks, ranks)
        for d in range(0, devices, 2):
            up_out[m, :, pl.ds(d * features, 2 * features)] = jnp.concatenate(
                [got[d, row, lane], got[d + 1, row, lane]], axis=1
            )
        own = pl.ds(m * BLOCK, BLOCK)
        part[m] = dot(down_out[m], tok[own, :], ROW_ROW)
        part[blocks + m] = adapter_scale * dot(up_out[m], cot[own, at], ROW_ROW)


def tile_kernel(blocks, core_ref, part, other, tok, cot, out, low_out, back_out):
    devices, ranks, width = out.shape[0], part.shape[1], out.shape[2]
    columns = cot.shape[1] // 2
    features = columns // devices
    at = pl.ds(pl.multiple_of(core_ref[0] * columns, LANES), columns)
    summed = part[...] + other[...]
    ups = []
    for m in range(blocks):
        own = pl.ds(m * BLOCK, BLOCK)
        low = summed[m].astype(jnp.bfloat16)
        back = summed[blocks + m].astype(jnp.bfloat16)
        low_out[own, :] = jnp.transpose(summed[m]).astype(jnp.bfloat16)
        back_out[own, :] = jnp.transpose(summed[blocks + m]).astype(jnp.bfloat16)
        for d in range(devices):
            piece = dot(back, tok[own, pl.ds(d * width, width)])
            out[d, pl.ds(m * ranks, ranks), :] = piece.astype(out.dtype)
        ups.append(adapter_scale * dot(low, cot[own, at]))
    lanes = blocks * features
    for d in range(devices):
        piece = jnp.concatenate([u[:, d * features : (d + 1) * features] for u in ups], axis=1)
        out[d, pl.ds(blocks * ranks, ranks), pl.ds(0, lanes)] = piece.astype(out.dtype)
    rest = width - lanes
    out[:, pl.ds(blocks * ranks, ranks), pl.ds(lanes, rest)] = jnp.zeros(
        (devices, ranks, rest), out.dtype
    )


def spread_kernel(blocks, ids, ids_column, got, down_out, up_out, scratch):
    step = pl.program_id(0)
    many, ranks = down_out.shape[0], down_out.shape[1]
    devices = got.shape[0]
    down_out[...] = jnp.zeros(down_out.shape, down_out.dtype)
    for i in range(devices * blocks):
        where = ids[i] - step * many

        @pl.when((where >= 0) & (where < many))
        def _():
            tile = got[i // blocks, pl.ds(i % blocks * ranks, ranks), :].astype(jnp.float32)
            down_out[where] = down_out[where] + tile

    @pl.when(step == 0)
    def _():
        count = up_out.shape[1]
        features = up_out.shape[0] // ranks
        scratch[...] = got[:, pl.ds(blocks * ranks, ranks), pl.ds(0, blocks * features)].astype(
            jnp.float32
        )
        chosen = [one_hot(ids_column[pl.ds(m * devices, devices), :], count) for m in range(blocks)]
        for r in range(ranks):
            turned = jnp.transpose(scratch[:, r, :]).astype(jnp.bfloat16)
            total = 0.0
            for m in range(blocks):
                total = total + dot(turned[m * features : (m + 1) * features], chosen[m])
            up_out[pl.ds(r * features, features), :] = total


def kv_pair_kernel(keep, got, out):
    rows = out.shape[0]
    lower = pl.ds(rows, rows)
    out[...] = (keep[lower, :] + got[lower, :].astype(jnp.float32)).astype(out.dtype)


def kv_kernel(keep, core_got, pair_got, low, up, out):
    rows = out.shape[0]
    for m in range(rows // BLOCK):
        own = pl.ds(m * BLOCK, BLOCK)
        base = keep[own, :] + core_got[own, :].astype(jnp.float32)
        base = base + pair_got[own, :].astype(jnp.float32)
        adapter = adapter_scale * dot(low[own, :], up[m])
        adapter = adapter.astype(jnp.bfloat16).astype(jnp.float32)
        out[own, :] = (base + adapter).astype(out.dtype)


def finish_kernel(starts, half, own, place, *refs):
    count = len(starts)
    sums, (back, down), refs = refs[:count], refs[count : count + 2], refs[count + 2 :]
    out, finished, sems = refs[-3:]
    x = place[0] if own else 1 - place[0]
    base = pl.multiple_of(x * half, LANES)
    copies = []
    for i, start in enumerate(starts):
        depth = sums[i].shape[1]
        at = pl.ds(pl.multiple_of(base + start, LANES), depth)
        for m in range(down.shape[0]):
            rows = pl.ds(m * BLOCK, BLOCK)
            adapter = dot(back[rows, :], down[m, :, at]).astype(jnp.bfloat16)
            both = sums[i][rows, :].astype(jnp.float32) + adapter.astype(jnp.float32)
            finished[rows, pl.ds(start, depth)] = both.astype(finished.dtype)
        copies.append(
            pltpu.make_async_copy(finished.at[:, pl.ds(start, depth)], out.at[:, at], sems.at[i])
        )
        copies[-1].start()
    for copy in copies:
        copy.wait()


def finish(starts, place, sums, back, down, out):
    rows = sums[0].shape[0]
    half = sum(piece.shape[1] for piece in sums)
    ranks = down.shape[1]
    operands = [place, *sums, back, down]
    specs = [SMEM] + [VMEM] * (len(operands) - 1)
    aliases = {}
    if out is not None:
        aliases[len(operands)] = 0
        operands.append(out)
        specs.append(ANYWHERE)
    return pl.pallas_call(
        functools.partial(finish_kernel, starts, half, out is None),
        out_shape=jax.ShapeDtypeStruct((rows, 2 * half), jnp.bfloat16),
        in_specs=specs,
        out_specs=ANYWHERE,
        input_output_aliases=aliases,
        scratch_shapes=[
            pltpu.VMEM((rows, half), jnp.bfloat16),
            pltpu.SemaphoreType.DMA((len(starts),)),
        ],
        cost_estimate=cost(2 * rows * ranks * half, 8 * rows * half),
        compiler_params=LIMIT,
    )(*operands)


def paired(tokens, frozen_weight, cotangent, block_adapter_index, down_weight, up_weight):
    batches, batch_rows, shard = tokens.shape
    total = cotangent.shape[2]
    columns = total // 2
    rows = batches * batch_rows
    half = shard // 2
    tok = tokens.reshape(rows, shard)
    cot = cotangent.reshape(rows, total)
    adapters, down_rows, ranks = down_weight.shape
    features = up_weight.shape[2]
    per_device = batch_rows // BLOCK
    blocks = batches * per_device
    count = lax.axis_size("fsdp")
    layers = count // 4
    index = lax.axis_index("fsdp")
    core = lax.axis_index("tp")
    x, y, z = index % 2, (index // 2) % 2, index // 4
    bf16, f32 = jnp.bfloat16, jnp.float32
    shape = jax.ShapeDtypeStruct

    def move(axis, width, route, value):
        return send(value, axis, width, route)

    x_send = lambda v: move("fsdp", count, lambda i: i ^ 1, v)
    y_send = lambda v: move("fsdp", count, lambda i: i ^ 2, v)
    z_send = lambda v: move("fsdp", count, lambda i: (i + 4) % count, v)
    core_send = lambda v: move("tp", 2, lambda i: i ^ 1, v)

    chunks = ((0, half // 2), (half // 2, half // 2))
    block = frozen_weight.shape[1]
    here = jnp.stack([x, core]).astype(jnp.int32)
    split = chunks[1][0]
    theirs = [
        pl.pallas_call(
            functools.partial(first_kernel, 0, half),
            name="first",
            out_shape=shape((split, block), bf16),
            in_specs=[SMEM, ANYWHERE],
            out_specs=VMEM,
            scratch_shapes=[pltpu.SemaphoreType.DMA],
            cost_estimate=cost(0, 4 * split * block),
            compiler_params=LIMIT,
        )(here, frozen_weight)
    ]
    mine, later, tok_sent, cot_sent = pl.pallas_call(
        functools.partial(prep_kernel, split),
        name="prep",
        out_shape=(
            shape((half, block), bf16),
            shape((half - split, block), bf16),
            shape((rows, half), bf16),
            shape((rows, columns), bf16),
        ),
        in_specs=[SMEM, ANYWHERE, ANYWHERE, ANYWHERE],
        out_specs=(VMEM,) * 4,
        scratch_shapes=[pltpu.SemaphoreType.DMA((4,))],
        cost_estimate=cost(0, 4 * (2 * half * block + rows * (half + columns))),
        compiler_params=LIMIT,
    )(here, frozen_weight, tok, cot)
    theirs.append(later)
    mine_y = y_send(mine)
    tok_pair = x_send(tok_sent)
    cot_part = x_send(cot_sent)
    cot_rest = core_send(cot_part)
    held, theirs_y = [], []
    for c, (start, depth) in enumerate(chunks):
        got = x_send(theirs[c])
        held.append(
            pl.pallas_call(
                functools.partial(pair_kernel, start),
                out_shape=shape((depth, 2 * block), bf16),
                in_specs=[SMEM, VMEM, VMEM],
                out_specs=VMEM,
                cost_estimate=cost(0, 8 * depth * block),
                compiler_params=LIMIT,
            )(here, mine, got)
        )
        theirs_y.append(y_send(got))

    ids = (
        block_adapter_index.reshape(batches, count, per_device)
        .transpose(1, 0, 2)
        .reshape(count, blocks)
    )
    id_list = ids.reshape(-1)
    id_column = ids.T.reshape(-1, 1)

    def exchange(value):
        return lax.all_to_all(value, "fsdp", split_axis=0, concat_axis=0, tiled=True)

    packet = shape((count, (blocks + 1) * ranks, down_rows), bf16)
    packet_bytes = 2 * count * (blocks + 1) * ranks * down_rows
    parcel = pl.pallas_call(
        functools.partial(fetch_kernel, blocks),
        name="fetch",
        out_shape=packet,
        in_specs=[SMEM, VMEM, ANYWHERE, VMEM],
        out_specs=VMEM,
        scratch_shapes=[
            pltpu.VMEM((count, ranks, blocks * features), f32),
            pltpu.SemaphoreType.DMA((count * blocks,)),
        ],
        cost_estimate=cost(0, 4 * packet_bytes),
        compiler_params=LIMIT,
    )(
        id_list,
        id_column,
        down_weight.transpose(0, 2, 1),
        up_weight.transpose(1, 2, 0).reshape(ranks * features, adapters),
    )
    arrived = exchange(parcel)
    core_place = core.astype(jnp.int32).reshape(1)
    down_mine, up_mine, part = pl.pallas_call(
        functools.partial(project_kernel, blocks),
        name="project",
        out_shape=(
            shape((blocks, ranks, shard), bf16),
            shape((blocks, ranks, columns), bf16),
            shape((2 * blocks, ranks, BLOCK), f32),
        ),
        in_specs=[SMEM, VMEM, VMEM, VMEM],
        out_specs=(VMEM, VMEM, VMEM),
        cost_estimate=cost(2 * rows * ranks * (shard + columns), 2 * rows * (shard + total)),
        compiler_params=LIMIT,
    )(core_place, arrived, tok, cot)
    other = core_send(part)
    tiles, low_rank, back_rank = pl.pallas_call(
        functools.partial(tile_kernel, blocks),
        name="tiles",
        out_shape=(packet, shape((rows, ranks), bf16), shape((rows, ranks), bf16)),
        in_specs=[SMEM, VMEM, VMEM, VMEM, VMEM],
        out_specs=(VMEM, VMEM, VMEM),
        cost_estimate=cost(2 * rows * ranks * (shard + columns), 2 * rows * (shard + total)),
        compiler_params=LIMIT,
    )(core_place, part, other, tok, cot)
    owned = exchange(tiles)
    many = adapters // 8
    grad_down, grad_up = pl.pallas_call(
        functools.partial(spread_kernel, blocks),
        name="spread",
        grid=(adapters // many,),
        out_shape=(
            shape((adapters, ranks, down_rows), f32),
            shape((ranks * features, adapters), f32),
        ),
        in_specs=[SMEM, VMEM, VMEM],
        out_specs=(
            pl.BlockSpec((many, ranks, down_rows), lambda i: (i, 0, 0)),
            pl.BlockSpec((ranks * features, adapters), lambda i: (0, 0)),
        ),
        scratch_shapes=[pltpu.VMEM((count, ranks, blocks * features), f32)],
        cost_estimate=cost(0, 4 * adapters * ranks * (down_rows + features)),
        compiler_params=LIMIT,
    )(id_list, id_column, owned)

    kv = None
    got_pieces, own_pieces = [], []
    for c, ((start, depth), own) in enumerate(zip(chunks, held)):
        arrays = [own, mine_y, theirs_y[c]]
        plan = [((0, 0, WHOLE),), ((1, start, MINE), (2, 0, THEIRS))]
        places = [z * 2 + y, z * 2 + 1 - y]
        for step in range(1, layers):
            own = z_send(own)
            layer = (z - step) % layers
            places += [layer * 2 + y, layer * 2 + 1 - y]
            plan += [((len(arrays), 0, WHOLE),), ((len(arrays) + 1, 0, WHOLE),)]
            arrays += [own, y_send(own)]
        last = start + depth == half
        places = jnp.stack(places + [x, core]).astype(jnp.int32)
        rows_of = (tok, tok_pair, cot, cot_part, cot_rest)

        def product(modes, kv):
            return chunk_product(
                places, tuple(plan), arrays, *rows_of, kv, start, depth, last, modes
            )

        if last:
            own_sum, pair = product(("ig",), None)
            results = product(("kv",), kv)
        else:
            own_sum, pair, kv = product(("kv", "ig"), kv)
        own_pieces.append(own_sum)
        got_pieces.append(x_send(pair))
    keep, other_columns = results
    core_got = core_send(other_columns)
    pair_sum = pl.pallas_call(
        kv_pair_kernel,
        name="kv_pair",
        out_shape=shape((rows, columns), bf16),
        in_specs=[VMEM, VMEM],
        out_specs=VMEM,
        cost_estimate=cost(0, 12 * rows * columns),
        compiler_params=LIMIT,
    )(keep, core_got)
    pair_got = x_send(pair_sum)
    key_value = pl.pallas_call(
        kv_kernel,
        name="kv_end",
        out_shape=shape((rows, columns), bf16),
        in_specs=[VMEM] * 5,
        out_specs=VMEM,
        cost_estimate=cost(2 * rows * ranks * columns, 12 * rows * columns),
        compiler_params=LIMIT,
    )(keep, core_got, pair_got, low_rank, up_mine)
    starts = tuple(start for start, _ in chunks)
    out = finish(starts, here, own_pieces, back_rank, down_mine, None)
    out = finish(starts, here, got_pieces, back_rank, down_mine, out)
    return (
        key_value.reshape(batches, batch_rows, columns),
        out.reshape(batches, batch_rows, shard),
        grad_down.transpose(0, 2, 1),
        grad_up.reshape(ranks, features, adapters).transpose(2, 0, 1),
    )


def selected_sum(adapter_selector, tiles):
    flat = tiles.reshape(tiles.shape[0], -1)
    return lax.dot_general(
        adapter_selector,
        flat,
        (((0,), (0,)), ((), ())),
        precision=lax.Precision.HIGHEST,
        preferred_element_type=jnp.float32,
    )


def plain(tokens, frozen_weight, cotangent, block_adapter_index, down_weight, up_weight):
    microbatch_list, token_block_rows, shard_width = tokens.shape
    kv_width = cotangent.shape[2]
    key_value_slice = kv_width // lax.axis_size("tp")
    row_total = microbatch_list * token_block_rows
    tok_matrix = tokens.reshape(row_total, shard_width)
    cot_matrix = cotangent.reshape(row_total, kv_width)
    adapter_number = down_weight.shape[0]
    rank_width = down_weight.shape[2]
    adapter_range = jnp.arange(adapter_number, dtype=jnp.int32)
    gathered = lax.all_gather(frozen_weight, "fsdp", axis=1, tiled=True)
    kv_partial = jnp.dot(tok_matrix, gathered, preferred_element_type=jnp.float32)
    frozen_key_value = lax.psum_scatter(kv_partial, "tp", scatter_dimension=1, tiled=True)
    frozen_input_gradient = lax.dot_general(
        cot_matrix, gathered, (((1,), (1,)), ((), ())), preferred_element_type=jnp.float32
    )
    cot_slab = lax.dynamic_slice_in_dim(
        cotangent, lax.axis_index("tp") * key_value_slice, key_value_slice, 2
    )
    fsdp_count = lax.axis_size("fsdp")
    per_dev = token_block_rows // BLOCK
    dest_ids = (
        block_adapter_index.reshape(microbatch_list, fsdp_count, per_dev)
        .transpose(1, 0, 2)
        .reshape(fsdp_count, microbatch_list * per_dev)
    )
    down_send = jnp.take(down_weight, dest_ids, axis=0).transpose(0, 1, 3, 2)
    up_send = jnp.take(up_weight, dest_ids, axis=0)
    down_mine, up_mine = (
        lax.all_to_all(down_send, "fsdp", split_axis=0, concat_axis=3, tiled=True),
        lax.all_to_all(up_send, "fsdp", split_axis=0, concat_axis=3, tiled=True),
    )
    down_mine = down_mine.reshape(microbatch_list, per_dev, rank_width, shard_width)
    up_mine = up_mine.reshape(microbatch_list, per_dev, rank_width, key_value_slice)
    tok_blocks = tokens.reshape(microbatch_list, per_dev, BLOCK, shard_width)
    gradient_blocks = cot_slab.reshape(microbatch_list, per_dev, BLOCK, key_value_slice)
    low_part = jnp.einsum(
        "mnbc,mnrc->mnbr", tok_blocks, down_mine, preferred_element_type=jnp.float32
    )
    partial_input_gradient = adapter_scale * jnp.einsum(
        "fsvj,fsyj->fsvy", gradient_blocks, up_mine, preferred_element_type=jnp.float32
    )
    low_sum, back_sum = lax.psum((low_part, partial_input_gradient), "tp")
    low_rank = low_sum.astype(jnp.bfloat16)
    rank_gradient = back_sum.astype(jnp.bfloat16)
    adapter_key_value = (
        adapter_scale
        * jnp.einsum("elui,elis->elus", low_rank, up_mine, preferred_element_type=jnp.float32)
    ).astype(jnp.bfloat16)
    adapter_input_gradient = jnp.einsum(
        "mnbr,mnrc->mnbc", rank_gradient, down_mine, preferred_element_type=jnp.float32
    ).astype(jnp.bfloat16)
    adapter_key_value = adapter_key_value.reshape(
        microbatch_list, token_block_rows, key_value_slice
    )
    adapter_input_gradient = adapter_input_gradient.reshape(
        microbatch_list, token_block_rows, shard_width
    )
    down_tiles = jnp.einsum(
        "mnbc,mnbr->mnrc", tok_blocks, rank_gradient, preferred_element_type=jnp.float32
    )
    up_weight_tiles = adapter_scale * jnp.einsum(
        "puai,puac->puic", low_rank, gradient_blocks, preferred_element_type=jnp.float32
    )
    down_tiles = down_tiles.reshape(microbatch_list * per_dev, rank_width, shard_width)
    up_weight_tiles = up_weight_tiles.reshape(
        microbatch_list * per_dev, rank_width, key_value_slice
    )
    down_owned, up_owned = (
        lax.all_to_all(
            down_tiles.astype(jnp.bfloat16), "fsdp", split_axis=2, concat_axis=0, tiled=True
        ).astype(down_tiles.dtype),
        lax.all_to_all(
            up_weight_tiles.astype(jnp.bfloat16), "fsdp", split_axis=2, concat_axis=0, tiled=True
        ).astype(up_weight_tiles.dtype),
    )
    owned_ids = dest_ids.reshape(-1)
    adapter_selector = (owned_ids[:, None] == adapter_range[None, :]).astype(jnp.float32)
    grad_down = (
        selected_sum(adapter_selector, down_owned)
        .reshape(adapter_number, rank_width, down_weight.shape[1])
        .transpose(0, 2, 1)
    )
    up_weight_gradient = selected_sum(adapter_selector, up_owned).reshape(up_weight.shape)
    key_value_output = (
        frozen_key_value.reshape(microbatch_list, token_block_rows, key_value_slice)
        + adapter_key_value.astype(jnp.float32)
    ).astype(jnp.bfloat16)
    input_gradient = (
        frozen_input_gradient.reshape(microbatch_list, token_block_rows, shard_width)
        + adapter_input_gradient.astype(jnp.float32)
    ).astype(jnp.bfloat16)
    return (key_value_output, input_gradient, grad_down, up_weight_gradient)


def local(tokens, frozen_weight, cotangent, block_adapter_index, down_weight, up_weight):
    batches, batch_rows, shard = tokens.shape
    blocks = batches * (batch_rows // BLOCK)
    features = up_weight.shape[2]
    fits = (
        lax.axis_size("tp") == 2
        and lax.axis_size("fsdp") % 4 == 0
        and frozen_weight.shape[1] % LANES == 0
        and shard % (16 * 2 * LANES) == 0
        and blocks * features == LANES
        and 2 * features == LANES
        and down_weight.shape[1] > LANES
        and down_weight.shape[0] % (8 * LANES // 2) == 0
    )
    body = paired if fits else plain
    return body(tokens, frozen_weight, cotangent, block_adapter_index, down_weight, up_weight)


def solution(mesh):
    return jax.shard_map(
        local,
        mesh=mesh,
        in_specs=(
            P(None, "fsdp", "tp"),
            P("tp", "fsdp"),
            P(None, "fsdp", None),
            P(),
            P(None, ("tp", "fsdp"), None),
            P(None, None, ("tp", "fsdp")),
        ),
        out_specs=(
            P(None, "fsdp", "tp"),
            P(None, "fsdp", "tp"),
            P(None, ("tp", "fsdp"), None),
            P(None, None, ("tp", "fsdp")),
        ),
        check_vma=False,
    )
```
